32 devices in a mesh: region: 2 (over y), cells: 16 (over z, x, core).
Axes of the slice: x: 2, y: 2, z: 4, core: 2. Of those that a mesh axis runs over, the one named last changes fastest.
Arguments:
- attributes: bfloat16 [32, 16384], P(None, ('region', 'cells')), may hold values from -6 to 6
- precip: bfloat16 [24, 16384], P(None, ('region', 'cells')), may hold values from 0.0099487305 to 3
- pet_demand: bfloat16 [24, 16384], P(None, ('region', 'cells')), may hold values from 0 to 1
- inflow_reach: int32 [16384], P(('region', 'cells')), may hold values from 0 to 191
- w_in: bfloat16 [32, 128], replicated, may hold values from -1 to 1
- w_hid: bfloat16 [2, 128, 128], replicated, may hold values from -0.5 to 0.5
- w_out: bfloat16 [128, 4], replicated, may hold values from -0.5 to 0.5
- block_inverse: float32 [4096, 128], P(('region', 'cells')), may hold values from -0.10606602 to 1
- upstream_coupling: float32 [4096, 128], P(('region', 'cells')), may hold values from -0.45078057 to 0.45078057
- discharge_cotangent: float32 [24, 4096], P(None, ('region', 'cells')), may hold values from -6 to 6
Outputs:
- discharge: float32 [24, 4096], P(None, ('region', 'cells'))
- grad_in: float32 [32, 128], replicated
- grad_hid: float32 [2, 128, 128], replicated
- grad_out: float32 [128, 4], replicated
The draws below stay inside these ranges and needn't reach their ends.
Inputs may be any that keep to these rules, and one draw needn't show every extreme that they name: `inflow_reach`: values of 128 or more mark padded rows of a tile, which carry no runoff to any reach.
All inputs are finite; a program needn't handle non-finite values.
Results may differ from the reference program's by a relative error of at most 0.022.
Values may be sent and summed in bfloat16 or wider, within the bound.
No kernel may reach another device: no remote copies, remote signals or barrier semaphores. Data moves between devices by JAX's collectives and lax.ppermute only.
A program may use at most 64 MiB of HBM per device.

```python
import math
import jax
import jax.numpy as jnp
from jax import lax

ATTR = 32
HID = 128
LAYERS = 2
PARAMS = 4
HOURS = 24
SLOT = 32
R_DEV = 128
CELL_DEV = 512
CELLS = 16384
R_TOTAL = 4096
N_REGION = 2
N_CELLS = 16


def draw_block_inverse(key, part):
    first, second = jax.random.split(jax.random.fold_in(key, 11))
    noise = jnp.clip(jax.random.normal(first, (R_TOTAL, R_DEV), jnp.float32), -4.0, 4.0) * (0.3 / R_DEV ** 0.5)
    diagonal = jax.random.uniform(second, (R_TOTAL, 1), jnp.float32, 0.5, 1.0)
    placed = jnp.arange(R_TOTAL)[:, None] % R_DEV == jnp.arange(R_DEV)[None, :]
    return jnp.where(placed, diagonal, noise)


def plant(array, stream_key, least, largest):
    longest = array.shape.index(max(array.shape))
    spots = []
    for shift in (0, 1):
        where = [jax.random.randint(jax.random.fold_in(stream_key, axis), (), 0, length) for axis, length in enumerate(array.shape)]
        where[longest] = (where[longest] + shift) % array.shape[longest]
        spots.append(tuple(where))
    return array.at[spots[0]].set(least).at[spots[1]].set(largest)


def block_scale(rng, extent, cuts, smallest, high):
    factor_of, own = 1.0, jax.random.fold_in(rng, 6)
    for position, blocks in cuts:
        draws = jnp.exp(jax.random.uniform(jax.random.fold_in(own, position), (blocks,), jnp.float32, smallest / len(cuts), high / len(cuts)))
        factor_of = factor_of * jnp.repeat(draws, extent[position] // blocks).reshape([-1 if axis == position else 1 for axis in range(len(extent))])
    return factor_of


def gaussian(key, shape, width, limit, cuts=(), kind=jnp.bfloat16):
    values = jax.random.normal(key, shape, jnp.float32) * width
    if len(cuts) > 0:
        values = block_scale(key, shape, cuts, -0.22, 0.18) * values
    return jnp.clip(values, min=-limit, max=limit).astype(kind)


def setup_inputs(seed: int = 0) -> dict:
    seeds = jax.random.split(jax.random.key(seed), 11)
    attributes = gaussian(seeds[0], (ATTR, CELLS), 1.0, 6.0, ((1, 32),))
    precip = jnp.clip(jnp.exp(math.log(3.0) - 5.7089226 * jax.random.uniform(seeds[1], (HOURS, CELLS), jnp.float32) ** block_scale(seeds[1], (HOURS, CELLS), ((1, 32),), -0.2, 0.2)), 0.0099487305, 3.0).astype(jnp.bfloat16)
    pet_demand = jnp.clip(1.0 * jax.random.uniform(seeds[2], (HOURS, CELLS), jnp.float32) ** block_scale(seeds[2], (HOURS, CELLS), ((1, 32),), -0.2, 0.2), 0.0, 1.0).astype(jnp.bfloat16)
    inflow_reach = plant(jax.random.randint(seeds[3], (CELLS,), 0, R_DEV + R_DEV // 2), jax.random.fold_in(seeds[3], 1), 0, (R_DEV + R_DEV // 2) - 1).astype(jnp.int32)
    w_in = gaussian(seeds[4], (ATTR, HID), ATTR ** -0.5, 1.0)
    w_hid = gaussian(seeds[5], (LAYERS, HID, HID), HID ** -0.5, 0.5)
    w_out = gaussian(seeds[6], (HID, PARAMS), HID ** -0.5, 0.5)
    block_inverse = draw_block_inverse(jax.random.fold_in(seeds[10], 71), 0)
    upstream_coupling = gaussian(seeds[8], (R_TOTAL, R_DEV), (0.85 / R_DEV ** 0.5), 0.45078057, ((0, 32),), jnp.float32)
    discharge_cotangent = gaussian(seeds[9], (HOURS, R_TOTAL), 1.0, 6.0, ((1, 32),), jnp.float32)
    return dict(attributes=attributes, precip=precip, pet_demand=pet_demand, inflow_reach=inflow_reach, w_in=w_in, w_hid=w_hid, w_out=w_out, block_inverse=block_inverse, upstream_coupling=upstream_coupling, discharge_cotangent=discharge_cotangent)


def land_model(attributes, w_in, w_hid, w_out, precip, pet_demand):
    hidden = jnp.tanh(jnp.dot(w_in.T, attributes, preferred_element_type=jnp.float32)).astype(jnp.bfloat16)
    for layer in range(w_hid.shape[0]):
        hidden = jnp.tanh(jnp.dot(w_hid[layer].T, hidden, preferred_element_type=jnp.float32)).astype(jnp.bfloat16)
    params = jnp.dot(w_out.T, hidden, preferred_element_type=jnp.float32)
    drain_rate = 0.02 + 0.3 * jax.nn.sigmoid(params[0])
    capacity = 1.0 + 4.0 * jax.nn.sigmoid(params[1])
    evap_rate = 0.3 * jax.nn.sigmoid(params[2])
    storage = jax.nn.sigmoid(params[3]) * capacity

    def hourly(storage, inputs):
        rain, demand = inputs
        storage = storage + rain
        spill = jax.nn.softplus(storage - capacity)
        storage = storage - spill
        drained = drain_rate * storage
        storage = storage - drained - evap_rate * demand * storage
        return (storage, spill + drained)
    final, runoff = lax.scan(hourly, storage, (precip.astype(jnp.float32), pet_demand.astype(jnp.float32)))
    return runoff.astype(jnp.bfloat16)

def one_hot_table(reach_ids):
    return (reach_ids[:, None] == jnp.arange(R_DEV, dtype=jnp.int32)[None, :]).astype(jnp.bfloat16)

def regroup(blocks):
    shaped = blocks.reshape(N_REGION, N_CELLS, HOURS, N_CELLS, SLOT)
    return shaped.transpose(0, 3, 2, 1, 4).reshape(N_REGION * N_CELLS, HOURS, CELL_DEV)

def reference(attributes, precip, pet_demand, inflow_reach, w_in, w_hid, w_out, block_inverse, upstream_coupling, discharge_cotangent):
    devices = N_REGION * N_CELLS
    attr_dev = attributes.reshape(ATTR, devices, CELL_DEV).transpose(1, 0, 2)
    rain_dev = precip.reshape(HOURS, devices, CELL_DEV).transpose(1, 0, 2)
    demand_dev = pet_demand.reshape(HOURS, devices, CELL_DEV).transpose(1, 0, 2)
    reach_dev = inflow_reach.reshape(devices, CELL_DEV)
    lateral_scale = R_DEV / CELL_DEV
    runoff = lax.map(lambda item: land_model(item[0], w_in, w_hid, w_out, item[1], item[2]), (attr_dev, rain_dev, demand_dev))
    received = regroup(runoff)

    def lateral_of(item):
        return jnp.dot(item[0], one_hot_table(item[1]), preferred_element_type=jnp.float32) * lateral_scale
    lateral = lax.map(lateral_of, (received, reach_dev)).reshape(N_REGION, N_CELLS, HOURS, R_DEV)
    inverse = block_inverse.reshape(N_REGION, N_CELLS, R_DEV, R_DEV)
    coupling = upstream_coupling.reshape(N_REGION, N_CELLS, R_DEV, R_DEV)
    high = lax.Precision.HIGHEST
    flows = []
    previous = jnp.zeros((N_CELLS, HOURS, R_DEV), jnp.float32)
    for region in range(N_REGION):
        inflow = lateral[region] + jnp.einsum('nhr,nrk->nhk', previous, coupling[region], precision=high)
        previous = jnp.einsum('nhr,nrk->nhk', inflow, inverse[region], precision=high)
        flows.append(previous)
    discharge = jnp.stack(flows).transpose(2, 0, 1, 3).reshape(HOURS, N_REGION * N_CELLS * R_DEV)
    cotangent = discharge_cotangent.reshape(HOURS, N_REGION, N_CELLS, R_DEV).transpose(1, 2, 0, 3)
    carry = jnp.zeros((N_CELLS, HOURS, R_DEV), jnp.float32)
    adjoints = [None] * N_REGION
    for region in range(N_REGION - 1, -1, -1):
        lateral_ct = jnp.einsum('nhr,nkr->nhk', cotangent[region] + carry, inverse[region], precision=high)
        carry = jnp.einsum('nhr,nkr->nhk', lateral_ct, coupling[region], precision=high)
        adjoints[region] = lateral_ct
    lateral_ct = jnp.stack(adjoints).reshape(devices, HOURS, R_DEV)

    def cell_ct_of(item):
        scaled = (item[0] * lateral_scale).astype(jnp.bfloat16)
        table = one_hot_table(item[1])
        return lax.dot_general(scaled, table, (((1,), (1,)), ((), ())), preferred_element_type=jnp.float32).astype(jnp.bfloat16)
    received_ct = lax.map(cell_ct_of, (lateral_ct, reach_dev))
    runoff_ct = regroup(received_ct)

    def grads_of(item):

        def model_of(weights):
            return land_model(item[0], weights[0], weights[1], weights[2], item[1], item[2])
        result, pullback = jax.vjp(model_of, (w_in, w_hid, w_out))
        return pullback(item[3])[0]
    grads = lax.map(grads_of, (attr_dev, rain_dev, demand_dev, runoff_ct))
    grad_in = lax.optimization_barrier(jnp.sum(grads[0].astype(jnp.float32), axis=0)) / devices
    grad_hid = lax.optimization_barrier(jnp.sum(grads[1].astype(jnp.float32), axis=0)) / devices
    grad_out = lax.optimization_barrier(jnp.sum(grads[2].astype(jnp.float32), axis=0)) / devices
    return (discharge, grad_in, grad_hid, grad_out)
```

```python
import functools

import jax
import jax.numpy as jnp
from jax import lax
from jax.experimental import pallas as pl
from jax.experimental.pallas import tpu as pltpu
from jax.sharding import PartitionSpec as P

F32 = jnp.float32
BF16 = jnp.bfloat16
LANES = 128
VMEM = pl.BlockSpec(memory_space=pltpu.VMEM)
SMEM = pl.BlockSpec(memory_space=pltpu.SMEM)
NT = (((1,), (1,)), ((), ()))


def dot(left, right, dims=(((1,), (0,)), ((), ()))):
    return lax.dot_general(left, right, dims, preferred_element_type=F32)


def matmul_high(left, right):
    return jnp.dot(left, right, precision=lax.Precision.HIGHEST, preferred_element_type=F32)


def shifted(block, axis, distance):
    devices = range(lax.axis_size(axis))
    route = [(i - distance, i) for i in devices if i - distance in devices]
    return lax.ppermute(block, axis, route)


def swap_groups(group):
    lane = lax.broadcasted_iota(jnp.int32, group[0].shape, 1)
    half, quarter = LANES // 2, LANES // 4
    low = lane < half
    wide = [None] * 4
    for k in range(2):
        wide[k] = jnp.where(low, group[k], pltpu.roll(group[k + 2], half, 1))
        wide[k + 2] = jnp.where(low, pltpu.roll(group[k], half, 1), group[k + 2])
    even = lane % half < quarter
    out = [None] * 4
    for k in (0, 2):
        out[k] = jnp.where(even, wide[k], pltpu.roll(wide[k + 1], quarter, 1))
        out[k + 1] = jnp.where(even, pltpu.roll(wide[k], LANES - quarter, 1), wide[k + 1])
    return out


def pack_kernel(attr_ref, rain_ref, demand_ref, out_ref):
    hours, cells = rain_ref.shape
    half = attr_ref.shape[0] // 2
    attr = attr_ref[...].astype(F32)
    fill = jnp.zeros((hours - half, cells), F32)
    rows = [
        rain_ref[...].astype(F32),
        demand_ref[...].astype(F32),
        jnp.concatenate([attr[:half], fill], axis=0),
        jnp.concatenate([attr[half:], fill], axis=0),
    ]
    for column in range(cells // LANES):
        window = slice(column * LANES, (column + 1) * LANES)
        for k, block in enumerate(swap_groups([r[:, window] for r in rows])):
            out_ref[4 * column + k] = block.astype(BF16)


def main_kernel(
    core_ref,
    packed_ref,
    ct_ref,
    w_in_t_ref,
    w_hid_t_ref,
    w_hid_ref,
    w_out_t_ref,
    w_out_ref,
    runoff_ref,
    keep_ref,
    send_ref,
    rain_s,
    demand_s,
    attr_s,
    x_s,
    carry_s,
):
    hours, cells = rain_s.shape
    half = attr_s.shape[0] // 2
    for column in range(cells // LANES):
        window = slice(column * LANES, (column + 1) * LANES)
        rain, demand, first, second = swap_groups(
            [packed_ref[4 * column + k].astype(F32) for k in range(4)]
        )
        rain_s[:, window] = rain
        demand_s[:, window] = demand
        attr_s[:half, window] = first[:half]
        attr_s[half:, window] = second[:half]

    layers = w_hid_ref.shape[0]
    attr = attr_s[...].astype(BF16)
    wide = [jnp.tanh(dot(w_in_t_ref[...], attr))]
    hidden = [wide[0].astype(BF16)]
    for layer in range(layers):
        wide.append(jnp.tanh(dot(w_hid_t_ref[layer], hidden[-1])))
        hidden.append(wide[-1].astype(BF16))
    params = dot(w_out_t_ref[...], hidden[-1])
    gate = jax.nn.sigmoid(params)
    gate0, gate1, gate2, gate3 = (gate[i : i + 1] for i in range(4))
    drain = 0.02 + 0.3 * gate0
    capacity = 1.0 + 4.0 * gate1
    evap = 0.3 * gate2
    storage = gate3 * capacity

    demand = demand_s[...]
    kept = (1.0 - drain) - evap * demand
    carry_s[...] = kept
    rain_s[...] = rain_s[...] - capacity
    for hour in range(hours):
        x = storage + rain_s[hour : hour + 1]
        x_s[hour : hour + 1] = x
        under = jnp.maximum(-x, 0.0) + jnp.log(1.0 + jnp.exp(-jnp.abs(x)))
        storage = (capacity - under) * carry_s[hour : hour + 1]

    x = x_s[...]
    ct = ct_ref[...].astype(F32)
    small = jnp.exp(-jnp.abs(x))
    log = jnp.log(1.0 + small)
    spill = jnp.maximum(x, 0.0) + log
    level = capacity - (jnp.maximum(-x, 0.0) + log)
    runoff_ref[...] = (spill + drain * level).astype(BF16)
    share = 1.0 / (1.0 + small)
    slope = jnp.where(x >= 0.0, share, small * share)
    rest = 1.0 - slope
    x_s[...] = kept * rest
    rain_s[...] = ct * (drain * rest + slope)
    carry = jnp.zeros((1, cells), F32)
    for hour in range(hours - 1, -1, -1):
        carry_s[hour : hour + 1] = carry
        carry = carry * x_s[hour : hour + 1] + rain_s[hour : hour + 1]
    after = carry_s[...]
    level_ct = after * kept + ct * drain
    capacity_ct = -jnp.sum(slope * (ct - level_ct), axis=0, keepdims=True)
    held = after * level
    drain_ct = jnp.sum(level * ct - held, axis=0, keepdims=True)
    evap_ct = -jnp.sum(held * demand, axis=0, keepdims=True)
    capacity_ct = capacity_ct + carry * gate3
    params_ct = jnp.concatenate(
        [
            drain_ct * (0.3 * gate0 * (1.0 - gate0)),
            capacity_ct * (4.0 * gate1 * (1.0 - gate1)),
            evap_ct * (0.3 * gate2 * (1.0 - gate2)),
            carry * capacity * (gate3 * (1.0 - gate3)),
            jnp.zeros((4, cells), F32),
        ],
        axis=0,
    ).astype(BF16)

    grad_out = dot(params_ct, hidden[-1], NT)
    back = dot(w_out_ref[...], params_ct)
    grads = [None] * layers
    for layer in range(layers - 1, -1, -1):
        top = wide[layer + 1]
        g = (back * (1.0 - top * top)).astype(BF16)
        grads[layer] = dot(hidden[layer], g, NT)
        back = dot(w_hid_ref[layer], g)
    g = (back * (1.0 - wide[0] * wide[0])).astype(BF16)
    grad_in = dot(attr, g, NT)

    rows, width = keep_ref.shape
    fill = rows - grads[1].shape[0] - grad_out.shape[0]
    first = jnp.concatenate([grads[0], grad_in], axis=0)
    second = jnp.concatenate([grads[1], grad_out, jnp.zeros((fill, width), F32)], axis=0)
    lower = core_ref[0] == 0

    @pl.when(lower)
    def _():
        keep_ref[...] = first.astype(BF16)
        send_ref[...] = second.astype(BF16)

    @pl.when(jnp.logical_not(lower))
    def _():
        keep_ref[...] = second.astype(BF16)
        send_ref[...] = first.astype(BF16)


def finish_kernel(scale, core_ref, mine_ref, other_ref, grad_in_ref, grad_hid_ref, grad_out_ref):
    hid = grad_hid_ref.shape[1]
    params = grad_out_ref.shape[0]

    def place(first, second):
        grad_hid_ref[0] = first[:hid] * scale
        grad_in_ref[...] = first[hid:] * scale
        grad_hid_ref[1] = second[:hid] * scale
        grad_out_ref[...] = second[hid : hid + params] * scale

    lower = core_ref[0] == 0

    @pl.when(lower)
    def _():
        place(mine_ref, other_ref)

    @pl.when(jnp.logical_not(lower))
    def _():
        place(other_ref, mine_ref)


def exchange(block, region_flip, cells_flip):
    regions, cells = lax.axis_size("region"), lax.axis_size("cells")
    route = [
        (r * cells + c, (r ^ region_flip) * cells + (c ^ cells_flip))
        for r in range(regions)
        for c in range(cells)
    ]
    return lax.ppermute(block, ("region", "cells"), route)


def sum_over_devices(keep, send):
    regions, cells = lax.axis_size("region"), lax.axis_size("cells")
    total = keep.astype(F32) + exchange(send, 0, 1).astype(F32)
    bits = [(1 << b, 0) for b in range(regions.bit_length() - 1)]
    bits += [(0, 1 << b) for b in range(1, cells.bit_length() - 1)]
    while bits:
        pair, bits = bits[:2], bits[2:]
        block = total.astype(BF16)
        own = block.astype(F32)
        if len(pair) == 1:
            total = own + exchange(block, *pair[0]).astype(F32)
            continue
        (r0, c0), (r1, c1) = pair
        far = exchange(block, r0 ^ r1, c0 ^ c1).astype(F32)
        near = exchange(block, r0, c0).astype(F32)
        next_ = exchange(block, r1, c1).astype(F32)
        total = (own + near) + (next_ + far)
    return total, exchange(total, 0, 1)


def per_device(
    attributes,
    precip,
    pet_demand,
    inflow_reach,
    w_in,
    w_hid,
    w_out,
    block_inverse,
    upstream_coupling,
    discharge_cotangent,
):
    hours, cells = precip.shape
    regions, owners = lax.axis_size("region"), lax.axis_size("cells")
    attrs, hid = w_in.shape
    params = w_out.shape[1]
    reach_count = block_inverse.shape[1]
    lateral_scale = reach_count / cells
    core = (lax.axis_index("cells") % 2).astype(jnp.int32).reshape(1)

    packed = pl.pallas_call(
        pack_kernel,
        out_shape=jax.ShapeDtypeStruct((owners, hours, LANES), BF16),
        in_specs=[VMEM] * 3,
        out_specs=VMEM,
        name="pack",
    )(attributes, precip, pet_demand)
    arrived = lax.all_to_all(packed, "cells", split_axis=0, concat_axis=0, tiled=True)

    onehot = (inflow_reach[:, None] == jnp.arange(reach_count, dtype=jnp.int32)[None, :]).astype(
        BF16
    )
    inverse_t = block_inverse.T
    coupling_t = upstream_coupling.T
    lateral_ct = matmul_high(discharge_cotangent, inverse_t)
    for _ in range(regions - 1):
        incoming = shifted(matmul_high(lateral_ct, coupling_t), "region", -1)
        lateral_ct = matmul_high(discharge_cotangent + incoming, inverse_t)
    scaled_ct = (lateral_ct * lateral_scale).astype(BF16)
    received_ct = dot(scaled_ct, onehot, NT).astype(BF16)

    w_out_t = jnp.pad(w_out.T, ((0, 8 - params), (0, 0)))
    w_out_wide = jnp.pad(w_out, ((0, 0), (0, 8 - params)))
    rows = hid + attrs
    runoff, keep, send = pl.pallas_call(
        main_kernel,
        out_shape=(
            jax.ShapeDtypeStruct((hours, cells), BF16),
            jax.ShapeDtypeStruct((rows, hid), BF16),
            jax.ShapeDtypeStruct((rows, hid), BF16),
        ),
        in_specs=[SMEM] + [VMEM] * 7,
        out_specs=(VMEM, VMEM, VMEM),
        scratch_shapes=[
            pltpu.VMEM((hours, cells), F32),
            pltpu.VMEM((hours, cells), F32),
            pltpu.VMEM((attrs, cells), F32),
            pltpu.VMEM((hours, cells), F32),
            pltpu.VMEM((hours, cells), F32),
        ],
        compiler_params=pltpu.CompilerParams(vmem_limit_bytes=48 << 20),
        name="model",
    )(
        core,
        arrived,
        received_ct,
        w_in.T,
        jnp.swapaxes(w_hid, 1, 2),
        w_hid,
        w_out_t,
        w_out_wide,
    )

    mine, other = sum_over_devices(keep, send)

    lateral = dot(runoff, onehot) * lateral_scale
    discharge = matmul_high(lateral, block_inverse)
    for _ in range(regions - 1):
        incoming = shifted(discharge, "region", 1)
        discharge = matmul_high(
            lateral + matmul_high(incoming, upstream_coupling), block_inverse
        )

    grad_in, grad_hid, grad_out = pl.pallas_call(
        functools.partial(finish_kernel, 1.0 / (regions * owners)),
        out_shape=(
            jax.ShapeDtypeStruct((attrs, hid), F32),
            jax.ShapeDtypeStruct((2, hid, hid), F32),
            jax.ShapeDtypeStruct((params, hid), F32),
        ),
        in_specs=[SMEM, VMEM, VMEM],
        out_specs=(VMEM, VMEM, VMEM),
        name="finish",
    )(core, mine, other)
    return discharge, grad_in, grad_hid, grad_out.T


def solution(mesh):
    split = ("region", "cells")
    placed = (
        P(None, split),
        P(None, split),
        P(None, split),
        P(split),
        P(),
        P(),
        P(),
        P(split, None),
        P(split, None),
        P(None, split),
    )
    return jax.shard_map(
        per_device,
        mesh=mesh,
        in_specs=placed,
        out_specs=(P(None, split), P(), P(), P()),
        check_vma=False,
    )
```

```python
import functools

import jax
import jax.numpy as jnp
from jax import lax
from jax.experimental import pallas as pl
from jax.experimental.pallas import tpu as pltpu
from jax.sharding import PartitionSpec as P

F32 = jnp.float32
BF16 = jnp.bfloat16
LANES = 128
VMEM = pl.BlockSpec(memory_space=pltpu.VMEM)
HBM = pl.BlockSpec(memory_space=pltpu.HBM)
NT = (((1,), (1,)), ((), ()))


def dot(left, right, dims=(((1,), (0,)), ((), ()))):
    return lax.dot_general(left, right, dims, preferred_element_type=F32)


def dot_high(left, right, dims=(((1,), (0,)), ((), ()))):
    return lax.dot_general(
        left, right, dims, precision=lax.Precision.HIGHEST, preferred_element_type=F32
    )


def shifted(block, axis, distance):
    devices = range(lax.axis_size(axis))
    route = [(i - distance, i) for i in devices if i - distance in devices]
    return lax.ppermute(block, axis, route)


def swap_groups(group):
    lane = lax.broadcasted_iota(jnp.int32, group[0].shape, 1)
    half, quarter = LANES // 2, LANES // 4
    low = lane < half
    wide = [None] * 4
    for k in range(2):
        wide[k] = jnp.where(low, group[k], pltpu.roll(group[k + 2], half, 1))
        wide[k + 2] = jnp.where(low, pltpu.roll(group[k], half, 1), group[k + 2])
    even = lane % half < quarter
    out = [None] * 4
    for k in (0, 2):
        out[k] = jnp.where(even, wide[k], pltpu.roll(wide[k + 1], quarter, 1))
        out[k + 1] = jnp.where(even, pltpu.roll(wide[k], LANES - quarter, 1), wide[k + 1])
    return out


def open_kernel(
    attr_hbm,
    rain_hbm,
    demand_hbm,
    ct_hbm,
    inverse_hbm,
    coupling_hbm,
    packed_ref,
    start_ref,
    outgoing_ref,
    attr_s,
    rain_s,
    demand_s,
    ct_s,
    inverse_s,
    coupling_s,
    sems,
):
    pairs = [
        (rain_hbm, rain_s),
        (demand_hbm, demand_s),
        (attr_hbm, attr_s),
        (inverse_hbm, inverse_s),
        (ct_hbm, ct_s),
        (coupling_hbm, coupling_s),
    ]
    copies = [pltpu.make_async_copy(a, b, sems.at[i]) for i, (a, b) in enumerate(pairs)]
    for copy in copies:
        copy.start()
    hours, cells = rain_s.shape
    half = attr_s.shape[0] // 2
    for copy in copies:
        copy.wait()
    start = dot_high(ct_s[...], inverse_s[...], NT)
    start_ref[...] = start
    outgoing_ref[...] = dot_high(start, coupling_s[...], NT)
    attr = attr_s[...].astype(F32)
    fill = jnp.zeros((hours - half, cells), F32)
    rows = [
        rain_s[...].astype(F32),
        demand_s[...].astype(F32),
        jnp.concatenate([attr[:half], fill], axis=0),
        jnp.concatenate([attr[half:], fill], axis=0),
    ]
    for column in range(cells // LANES):
        window = slice(column * LANES, (column + 1) * LANES)
        for k, block in enumerate(swap_groups([r[:, window] for r in rows])):
            packed_ref[4 * column + k] = block.astype(BF16)


def cotangent_kernel(scale, start_ref, incoming_ref, inverse_ref, inflow_ref, received_ref):
    lateral_ct = start_ref[...] + dot_high(incoming_ref[...], inverse_ref[...], NT)
    scaled = (lateral_ct * scale).astype(BF16)
    shape = (scaled.shape[1], inflow_ref.shape[1])
    onehot = (
        jnp.broadcast_to(inflow_ref[...], shape) == lax.broadcasted_iota(jnp.int32, shape, 0)
    ).astype(F32)
    received_ref[...] = dot(scaled, onehot.astype(BF16)).astype(BF16)


def main_kernel(
    packed_ref,
    ct_ref,
    w_in_t_ref,
    w_hid_t_ref,
    w_hid_ref,
    w_out_t_ref,
    w_out_ref,
    runoff_ref,
    keep_ref,
    send_ref,
    rain_s,
    demand_s,
    attr_s,
    x_s,
    carry_s,
):
    hours, cells = rain_s.shape
    half = attr_s.shape[0] // 2
    for column in range(cells // LANES):
        window = slice(column * LANES, (column + 1) * LANES)
        rain, demand, first, second = swap_groups(
            [packed_ref[4 * column + k].astype(F32) for k in range(4)]
        )
        rain_s[:, window] = rain
        demand_s[:, window] = demand
        attr_s[:half, window] = first[:half]
        attr_s[half:, window] = second[:half]

    layers = w_hid_ref.shape[0]
    attr = attr_s[...].astype(BF16)
    wide = [jnp.tanh(dot(w_in_t_ref[...], attr))]
    hidden = [wide[0].astype(BF16)]
    for layer in range(layers):
        wide.append(jnp.tanh(dot(w_hid_t_ref[layer], hidden[-1])))
        hidden.append(wide[-1].astype(BF16))
    params = dot(w_out_t_ref[...], hidden[-1])
    gate = jax.nn.sigmoid(params)
    gate0, gate1, gate2, gate3 = (gate[i : i + 1] for i in range(4))
    drain = 0.02 + 0.3 * gate0
    capacity = 1.0 + 4.0 * gate1
    evap = 0.3 * gate2
    storage = gate3 * capacity

    demand = demand_s[...]
    kept = (1.0 - drain) - evap * demand
    carry_s[...] = kept
    rain_s[...] = rain_s[...] - capacity
    for hour in range(hours):
        x = storage + rain_s[hour : hour + 1]
        x_s[hour : hour + 1] = x
        under = jnp.maximum(-x, 0.0) + jnp.log(1.0 + jnp.exp(-jnp.abs(x)))
        storage = (capacity - under) * carry_s[hour : hour + 1]

    x = x_s[...]
    ct = ct_ref[...].astype(F32)
    small = jnp.exp(-jnp.abs(x))
    log = jnp.log(1.0 + small)
    spill = jnp.maximum(x, 0.0) + log
    level = capacity - (jnp.maximum(-x, 0.0) + log)
    runoff_ref[...] = (spill + drain * level).astype(BF16)
    share = 1.0 / (1.0 + small)
    slope = jnp.where(x >= 0.0, share, small * share)
    rest = 1.0 - slope
    x_s[...] = kept * rest
    rain_s[...] = ct * (drain * rest + slope)
    carry = jnp.zeros((1, cells), F32)
    for hour in range(hours - 1, -1, -1):
        carry_s[hour : hour + 1] = carry
        carry = carry * x_s[hour : hour + 1] + rain_s[hour : hour + 1]
    after = carry_s[...]
    level_ct = after * kept + ct * drain
    capacity_ct = -jnp.sum(slope * (ct - level_ct), axis=0, keepdims=True)
    held = after * level
    drain_ct = jnp.sum(level * ct - held, axis=0, keepdims=True)
    evap_ct = -jnp.sum(held * demand, axis=0, keepdims=True)
    capacity_ct = capacity_ct + carry * gate3
    params_ct = jnp.concatenate(
        [
            drain_ct * (0.3 * gate0 * (1.0 - gate0)),
            capacity_ct * (4.0 * gate1 * (1.0 - gate1)),
            evap_ct * (0.3 * gate2 * (1.0 - gate2)),
            carry * capacity * (gate3 * (1.0 - gate3)),
            jnp.zeros((4, cells), F32),
        ],
        axis=0,
    ).astype(BF16)

    grad_out = dot(params_ct, hidden[-1], NT)
    back = dot(w_out_ref[...], params_ct)
    grads = [None] * layers
    for layer in range(layers - 1, -1, -1):
        top = wide[layer + 1]
        g = (back * (1.0 - top * top)).astype(BF16)
        grads[layer] = dot(hidden[layer], g, NT)
        back = dot(w_hid_ref[layer], g)
    g = (back * (1.0 - wide[0] * wide[0])).astype(BF16)
    grad_in = dot(attr, g, NT)

    rows, width = keep_ref.shape
    fill = rows - grads[1].shape[0] - grad_out.shape[0]
    first = jnp.concatenate([grads[0], grad_in], axis=0)
    second = jnp.concatenate([grads[1], grad_out, jnp.zeros((fill, width), F32)], axis=0)
    lower = lax.axis_index("cells") & 1 == 0

    @pl.when(lower)
    def _():
        keep_ref[...] = first.astype(BF16)
        send_ref[...] = second.astype(BF16)

    @pl.when(jnp.logical_not(lower))
    def _():
        keep_ref[...] = second.astype(BF16)
        send_ref[...] = first.astype(BF16)


def finish_kernel(scale, mine_ref, other_ref, grad_in_ref, grad_hid_ref, grad_out_ref):
    hid = grad_hid_ref.shape[1]
    params = grad_out_ref.shape[0]

    def place(first, second):
        grad_hid_ref[0] = first[:hid] * scale
        grad_in_ref[...] = first[hid:] * scale
        grad_hid_ref[1] = second[:hid] * scale
        grad_out_ref[...] = second[hid : hid + params] * scale

    lower = lax.axis_index("cells") & 1 == 0

    @pl.when(lower)
    def _():
        place(mine_ref, other_ref)

    @pl.when(jnp.logical_not(lower))
    def _():
        place(other_ref, mine_ref)


def exchange(block, region_flip, cells_flip):
    regions, cells = lax.axis_size("region"), lax.axis_size("cells")
    route = [
        (r * cells + c, (r ^ region_flip) * cells + (c ^ cells_flip))
        for r in range(regions)
        for c in range(cells)
    ]
    return lax.ppermute(block, ("region", "cells"), route)


def per_device(
    attributes,
    precip,
    pet_demand,
    inflow_reach,
    w_in,
    w_hid,
    w_out,
    block_inverse,
    upstream_coupling,
    discharge_cotangent,
):
    hours, cells = precip.shape
    regions, owners = lax.axis_size("region"), lax.axis_size("cells")
    attrs, hid = w_in.shape
    params = w_out.shape[1]
    reach_count = block_inverse.shape[1]
    lateral_scale = reach_count / cells
    assert 4 * cells == LANES * owners and w_hid.shape[0] == 2
    assert regions & (regions - 1) == 0 and owners & (owners - 1) == 0
    shape = jax.ShapeDtypeStruct

    def in_hbm(array):
        return pltpu.with_memory_space_constraint(array, pltpu.HBM)

    packed, start_ct, outgoing = pl.pallas_call(
        open_kernel,
        out_shape=(
            shape((owners, hours, LANES), BF16),
            shape((hours, reach_count), F32),
            shape((hours, reach_count), F32),
        ),
        in_specs=[HBM] * 6,
        out_specs=(VMEM,) * 3,
        scratch_shapes=[
            pltpu.VMEM((attrs, cells), BF16),
            pltpu.VMEM((hours, cells), BF16),
            pltpu.VMEM((hours, cells), BF16),
            pltpu.VMEM((hours, reach_count), F32),
            pltpu.VMEM((reach_count, reach_count), F32),
            pltpu.VMEM((reach_count, reach_count), F32),
            pltpu.SemaphoreType.DMA((6,)),
        ],
        compiler_params=pltpu.CompilerParams(vmem_limit_bytes=8 << 20),
        name="open",
    )(
        in_hbm(attributes),
        in_hbm(precip),
        in_hbm(pet_demand),
        in_hbm(discharge_cotangent),
        in_hbm(block_inverse),
        in_hbm(upstream_coupling),
    )
    arrived = lax.all_to_all(packed, "cells", split_axis=0, concat_axis=0, tiled=True)

    incoming = jnp.zeros_like(start_ct)
    for step in range(regions - 1):
        if step:
            lateral_ct = start_ct + dot_high(incoming, block_inverse, NT)
            outgoing = dot_high(lateral_ct, upstream_coupling, NT)
        incoming = shifted(outgoing, "region", -1)
    received_ct = pl.pallas_call(
        functools.partial(cotangent_kernel, lateral_scale),
        out_shape=shape((hours, cells), BF16),
        in_specs=[VMEM] * 4,
        out_specs=VMEM,
        compiler_params=pltpu.CompilerParams(vmem_limit_bytes=8 << 20),
        name="cotangent",
    )(start_ct, incoming, block_inverse, inflow_reach.reshape(1, cells))

    w_out_t = jnp.pad(w_out.T, ((0, 8 - params), (0, 0)))
    w_out_wide = jnp.pad(w_out, ((0, 0), (0, 8 - params)))
    rows = hid + attrs
    runoff, keep, send = pl.pallas_call(
        main_kernel,
        out_shape=(
            shape((hours, cells), BF16),
            shape((rows, hid), BF16),
            shape((rows, hid), BF16),
        ),
        in_specs=[VMEM] * 7,
        out_specs=(VMEM, VMEM, VMEM),
        scratch_shapes=[
            pltpu.VMEM((hours, cells), F32),
            pltpu.VMEM((hours, cells), F32),
            pltpu.VMEM((attrs, cells), F32),
            pltpu.VMEM((hours, cells), F32),
            pltpu.VMEM((hours, cells), F32),
        ],
        compiler_params=pltpu.CompilerParams(vmem_limit_bytes=32 << 20),
        name="model",
    )(arrived, received_ct, w_in.T, jnp.swapaxes(w_hid, 1, 2), w_hid, w_out_t, w_out_wide)

    total = keep.astype(F32) + exchange(send, 0, 1).astype(F32)
    onehot = (inflow_reach[:, None] == jnp.arange(reach_count, dtype=jnp.int32)[None, :]).astype(
        BF16
    )
    lateral = dot(runoff, onehot) * lateral_scale
    discharge = dot_high(lateral, block_inverse)
    bits = [(1 << b, 0) for b in range(regions.bit_length() - 1)]
    bits += [(0, 1 << b) for b in range(1, owners.bit_length() - 1)]
    stages = [bits[k : k + 2] for k in range(0, len(bits), 2)]
    if regions != 2:
        for _ in range(regions - 1):
            incoming = shifted(discharge, "region", 1)
            discharge = dot_high(lateral + dot_high(incoming, upstream_coupling), block_inverse)
    for stage, pair in enumerate(stages):
        block = lax.optimization_barrier(total.astype(BF16))
        bundle = block
        if stage == 0 and regions == 2:
            upper = lax.reduce_precision(discharge, 8, 7)
            bundle = jnp.concatenate(
                [block, upper.astype(BF16), (discharge - upper).astype(BF16)], axis=0
            )
        first = exchange(bundle, *pair[0])
        parts = [block, first[:rows]]
        if len(pair) == 2:
            (r0, c0), (r1, c1) = pair
            parts += [exchange(block, r1, c1), exchange(block, r0 ^ r1, c0 ^ c1)]
        parts = [p.astype(F32) for p in parts]
        total = parts[0] + parts[1]
        if len(pair) == 2:
            total = total + (parts[2] + parts[3])
        if stage == 0 and regions == 2:
            upper, lower = first[rows : rows + hours], first[rows + hours :]
            incoming = upper.astype(F32) + lower.astype(F32)
            incoming = jnp.where(lax.axis_index("region") == 0, 0.0, incoming)
            discharge = dot_high(lateral + dot_high(incoming, upstream_coupling), block_inverse)
    other = exchange(total, 0, 1)

    grad_in, grad_hid, grad_out = pl.pallas_call(
        functools.partial(finish_kernel, 1.0 / (regions * owners)),
        out_shape=(
            shape((attrs, hid), F32),
            shape((2, hid, hid), F32),
            shape((params, hid), F32),
        ),
        in_specs=[VMEM, VMEM],
        out_specs=(VMEM, VMEM, VMEM),
        compiler_params=pltpu.CompilerParams(vmem_limit_bytes=4 << 20),
        name="finish",
    )(total, other)
    return discharge, grad_in, grad_hid, grad_out.T


def solution(mesh):
    split = ("region", "cells")
    placed = (
        P(None, split),
        P(None, split),
        P(None, split),
        P(split),
        P(),
        P(),
        P(),
        P(split, None),
        P(split, None),
        P(None, split),
    )
    return jax.shard_map(
        per_device,
        mesh=mesh,
        in_specs=placed,
        out_specs=(P(None, split), P(), P(), P()),
        check_vma=False,
    )
```

```python
import functools

import jax
import jax.numpy as jnp
from jax import lax
from jax.experimental import pallas as pl
from jax.experimental.pallas import tpu as pltpu
from jax.sharding import PartitionSpec as P

F32 = jnp.float32
BF16 = jnp.bfloat16
LANES = 128
VMEM = pl.BlockSpec(memory_space=pltpu.VMEM)
HBM = pl.BlockSpec(memory_space=pltpu.HBM)
NT = (((1,), (1,)), ((), ()))
TN = (((0,), (0,)), ((), ()))


def dot(left, right, dims=(((1,), (0,)), ((), ()))):
    return lax.dot_general(left, right, dims, preferred_element_type=F32)


def dot_high(left, right, dims=(((1,), (0,)), ((), ()))):
    return lax.dot_general(
        left, right, dims, precision=lax.Precision.HIGHEST, preferred_element_type=F32
    )


def shifted(block, axis, distance):
    devices = range(lax.axis_size(axis))
    route = [(i - distance, i) for i in devices if i - distance in devices]
    return lax.ppermute(block, axis, route)


def swap_groups(group):
    lane = lax.broadcasted_iota(jnp.int32, group[0].shape, 1)
    half, quarter = LANES // 2, LANES // 4
    low = lane < half
    wide = [None] * 4
    for k in range(2):
        wide[k] = jnp.where(low, group[k], pltpu.roll(group[k + 2], half, 1))
        wide[k + 2] = jnp.where(low, pltpu.roll(group[k], half, 1), group[k + 2])
    even = lane % half < quarter
    out = [None] * 4
    for k in (0, 2):
        out[k] = jnp.where(even, wide[k], pltpu.roll(wide[k + 1], quarter, 1))
        out[k + 1] = jnp.where(even, pltpu.roll(wide[k], LANES - quarter, 1), wide[k + 1])
    return out


def open_kernel(
    attr_hbm,
    rain_hbm,
    demand_hbm,
    ct_hbm,
    inverse_hbm,
    coupling_hbm,
    inflow_hbm,
    w_in_hbm,
    w_hid_hbm,
    w_out_hbm,
    packed_ref,
    ct_ref,
    inverse_ref,
    coupling_ref,
    inflow_ref,
    w_in_ref,
    w_hid_ref,
    w_out_ref,
    attr_s,
    rain_s,
    demand_s,
    w_out_s,
    sems,
):
    pairs = [
        (rain_hbm, rain_s),
        (demand_hbm, demand_s),
        (attr_hbm, attr_s),
        (inverse_hbm, inverse_ref),
        (ct_hbm, ct_ref),
        (coupling_hbm, coupling_ref),
        (w_out_hbm, w_out_s),
        (inflow_hbm, inflow_ref),
        (w_in_hbm, w_in_ref),
        (w_hid_hbm, w_hid_ref),
    ]
    copies = [pltpu.make_async_copy(a, b, sems.at[i]) for i, (a, b) in enumerate(pairs)]
    for copy in copies:
        copy.start()
    hours, cells = rain_s.shape
    half = attr_s.shape[0] // 2
    for copy in copies:
        copy.wait()
    out = w_out_s[...].astype(F32)
    wide = jnp.zeros((w_out_ref.shape[0] - out.shape[0], out.shape[1]), F32)
    w_out_ref[...] = jnp.concatenate([out, wide], axis=0).astype(BF16)
    attr = attr_s[...].astype(F32)
    fill = jnp.zeros((hours - half, cells), F32)
    rows = [
        rain_s[...].astype(F32),
        demand_s[...].astype(F32),
        jnp.concatenate([attr[:half], fill], axis=0),
        jnp.concatenate([attr[half:], fill], axis=0),
    ]
    for column in range(cells // LANES):
        window = slice(column * LANES, (column + 1) * LANES)
        for k, block in enumerate(swap_groups([r[:, window] for r in rows])):
            packed_ref[4 * column + k] = block.astype(BF16)


def adjoint_kernel(ct_ref, inverse_ref, coupling_ref, start_ref, outgoing_ref):
    start = dot_high(ct_ref[...], inverse_ref[...], NT)
    start_ref[...] = start
    outgoing_ref[...] = dot_high(start, coupling_ref[...], NT)


def cotangent_kernel(scale, start_ref, incoming_ref, inverse_ref, inflow_ref, received_ref):
    last = lax.axis_index("region") == lax.axis_size("region") - 1
    incoming = jnp.where(last, 0.0, incoming_ref[...])
    lateral_ct = start_ref[...] + dot_high(incoming, inverse_ref[...], NT)
    scaled = (lateral_ct * scale).astype(BF16)
    shape = (scaled.shape[1], inflow_ref.shape[1])
    onehot = (
        jnp.broadcast_to(inflow_ref[...], shape) == lax.broadcasted_iota(jnp.int32, shape, 0)
    ).astype(F32)
    received_ref[...] = dot(scaled, onehot.astype(BF16)).astype(BF16)


def main_kernel(
    packed_ref,
    ct_ref,
    w_in_ref,
    w_hid_ref,
    w_out_ref,
    runoff_ref,
    keep_ref,
    send_ref,
    rain_s,
    demand_s,
    attr_s,
    x_s,
    carry_s,
):
    hours, cells = rain_s.shape
    half = attr_s.shape[0] // 2
    for column in range(cells // LANES):
        window = slice(column * LANES, (column + 1) * LANES)
        rain, demand, first, second = swap_groups(
            [packed_ref[4 * column + k].astype(F32) for k in range(4)]
        )
        rain_s[:, window] = rain
        demand_s[:, window] = demand
        attr_s[:half, window] = first[:half]
        attr_s[half:, window] = second[:half]

    layers = w_hid_ref.shape[0]
    attr = attr_s[...].astype(BF16)
    wide = [jnp.tanh(dot(w_in_ref[...], attr, TN))]
    hidden = [wide[0].astype(BF16)]
    for layer in range(layers):
        wide.append(jnp.tanh(dot(w_hid_ref[layer], hidden[-1], TN)))
        hidden.append(wide[-1].astype(BF16))
    w_out = w_out_ref[...]
    params = dot(w_out, hidden[-1])[:8]
    gate = jax.nn.sigmoid(params)
    gate0, gate1, gate2, gate3 = (gate[i : i + 1] for i in range(4))
    drain = 0.02 + 0.3 * gate0
    capacity = 1.0 + 4.0 * gate1
    evap = 0.3 * gate2
    storage = gate3 * capacity

    demand = demand_s[...]
    kept = (1.0 - drain) - evap * demand
    carry_s[...] = kept
    rain_s[...] = rain_s[...] - capacity
    for hour in range(hours):
        x = storage + rain_s[hour : hour + 1]
        x_s[hour : hour + 1] = x
        under = jnp.maximum(-x, 0.0) + jnp.log(1.0 + jnp.exp(-jnp.abs(x)))
        storage = (capacity - under) * carry_s[hour : hour + 1]

    x = x_s[...]
    ct = ct_ref[...].astype(F32)
    small = jnp.exp(-jnp.abs(x))
    log = jnp.log(1.0 + small)
    spill = jnp.maximum(x, 0.0) + log
    level = capacity - (jnp.maximum(-x, 0.0) + log)
    runoff_ref[...] = (spill + drain * level).astype(BF16)
    share = 1.0 / (1.0 + small)
    slope = jnp.where(x >= 0.0, share, small * share)
    rest = 1.0 - slope
    x_s[...] = kept * rest
    rain_s[...] = ct * (drain * rest + slope)
    carry = jnp.zeros((1, cells), F32)
    for hour in range(hours - 1, -1, -1):
        carry_s[hour : hour + 1] = carry
        carry = carry * x_s[hour : hour + 1] + rain_s[hour : hour + 1]
    after = carry_s[...]
    level_ct = after * kept + ct * drain
    capacity_ct = -jnp.sum(slope * (ct - level_ct), axis=0, keepdims=True)
    held = after * level
    drain_ct = jnp.sum(level * ct - held, axis=0, keepdims=True)
    evap_ct = -jnp.sum(held * demand, axis=0, keepdims=True)
    capacity_ct = capacity_ct + carry * gate3
    params_ct = jnp.concatenate(
        [
            drain_ct * (0.3 * gate0 * (1.0 - gate0)),
            capacity_ct * (4.0 * gate1 * (1.0 - gate1)),
            evap_ct * (0.3 * gate2 * (1.0 - gate2)),
            carry * capacity * (gate3 * (1.0 - gate3)),
            jnp.zeros((w_out.shape[0] - 4, cells), F32),
        ],
        axis=0,
    ).astype(BF16)

    grad_out = dot(params_ct, hidden[-1], NT)
    back = dot(w_out, params_ct, TN)
    grads = [None] * layers
    for layer in range(layers - 1, -1, -1):
        top = wide[layer + 1]
        g = (back * (1.0 - top * top)).astype(BF16)
        grads[layer] = dot(hidden[layer], g, NT)
        back = dot(w_hid_ref[layer], g)
    g = (back * (1.0 - wide[0] * wide[0])).astype(BF16)
    grad_in = dot(attr, g, NT)

    rows, width = keep_ref.shape
    fill = rows - grads[1].shape[0] - grad_out.shape[0]
    first = jnp.concatenate([grads[0], grad_in], axis=0)
    second = jnp.concatenate([grads[1], grad_out, jnp.zeros((fill, width), F32)], axis=0)
    lower = lax.axis_index("cells") & 1 == 0

    @pl.when(lower)
    def _():
        keep_ref[...] = first.astype(BF16)
        send_ref[...] = second.astype(BF16)

    @pl.when(jnp.logical_not(lower))
    def _():
        keep_ref[...] = second.astype(BF16)
        send_ref[...] = first.astype(BF16)


def finish_kernel(scale, mine_ref, other_ref, grad_in_ref, grad_hid_ref, grad_out_ref):
    hid = grad_hid_ref.shape[1]
    params = grad_out_ref.shape[0]

    def place(first, second):
        grad_hid_ref[0] = first[:hid] * scale
        grad_in_ref[...] = first[hid:] * scale
        grad_hid_ref[1] = second[:hid] * scale
        grad_out_ref[...] = second[hid : hid + params] * scale

    lower = lax.axis_index("cells") & 1 == 0

    @pl.when(lower)
    def _():
        place(mine_ref, other_ref)

    @pl.when(jnp.logical_not(lower))
    def _():
        place(other_ref, mine_ref)


def exchange(block, region_flip, cells_flip):
    regions, cells = lax.axis_size("region"), lax.axis_size("cells")
    route = [
        (r * cells + c, (r ^ region_flip) * cells + (c ^ cells_flip))
        for r in range(regions)
        for c in range(cells)
    ]
    return lax.ppermute(block, ("region", "cells"), route)


def per_device(
    attributes,
    precip,
    pet_demand,
    inflow_reach,
    w_in,
    w_hid,
    w_out,
    block_inverse,
    upstream_coupling,
    discharge_cotangent,
):
    hours, cells = precip.shape
    regions, owners = lax.axis_size("region"), lax.axis_size("cells")
    attrs, hid = w_in.shape
    params = w_out.shape[1]
    reach_count = block_inverse.shape[1]
    lateral_scale = reach_count / cells
    assert 4 * cells == LANES * owners and w_hid.shape[0] == 2
    assert regions & (regions - 1) == 0 and owners & (owners - 1) == 0
    shape = jax.ShapeDtypeStruct

    def in_hbm(array):
        return pltpu.with_memory_space_constraint(array, pltpu.HBM)

    packed, ct, inverse, coupling, inflow, w_in_v, w_hid_v, w_out_v = pl.pallas_call(
        open_kernel,
        out_shape=(
            pltpu.VMEM((owners, hours, LANES), BF16),
            shape((hours, reach_count), F32),
            shape(block_inverse.shape, F32),
            shape(upstream_coupling.shape, F32),
            shape((1, cells), jnp.int32),
            shape(w_in.shape, BF16),
            shape(w_hid.shape, BF16),
            shape((16, hid), BF16),
        ),
        in_specs=[HBM] * 10,
        out_specs=(VMEM,) * 8,
        scratch_shapes=[
            pltpu.VMEM((attrs, cells), BF16),
            pltpu.VMEM((hours, cells), BF16),
            pltpu.VMEM((hours, cells), BF16),
            pltpu.VMEM((params, hid), BF16),
            pltpu.SemaphoreType.DMA((10,)),
        ],
        compiler_params=pltpu.CompilerParams(vmem_limit_bytes=8 << 20),
        name="open",
    )(
        in_hbm(attributes),
        in_hbm(precip),
        in_hbm(pet_demand),
        in_hbm(discharge_cotangent),
        in_hbm(block_inverse),
        in_hbm(upstream_coupling),
        in_hbm(inflow_reach.reshape(1, cells)),
        in_hbm(w_in),
        in_hbm(w_hid),
        in_hbm(w_out.T),
    )
    arrived = lax.all_to_all(packed, "cells", split_axis=0, concat_axis=0, tiled=True)

    start_ct, outgoing = pl.pallas_call(
        adjoint_kernel,
        out_shape=(shape((hours, reach_count), F32),) * 2,
        in_specs=[VMEM] * 3,
        out_specs=(VMEM,) * 2,
        compiler_params=pltpu.CompilerParams(vmem_limit_bytes=4 << 20),
        name="adjoint",
    )(ct, inverse, coupling)
    incoming = jnp.zeros_like(start_ct)
    for step in range(regions - 1):
        if step:
            lateral_ct = start_ct + dot_high(incoming, inverse, NT)
            outgoing = dot_high(lateral_ct, coupling, NT)
        if regions == 2:
            incoming = exchange(outgoing, 1, 0)
        else:
            incoming = shifted(outgoing, "region", -1)
    received_ct = pl.pallas_call(
        functools.partial(cotangent_kernel, lateral_scale),
        out_shape=shape((hours, cells), BF16),
        in_specs=[VMEM] * 4,
        out_specs=VMEM,
        compiler_params=pltpu.CompilerParams(vmem_limit_bytes=8 << 20),
        name="cotangent",
    )(start_ct, incoming, inverse, inflow)

    rows = hid + attrs
    runoff, keep, send = pl.pallas_call(
        main_kernel,
        out_shape=(
            shape((hours, cells), BF16),
            shape((rows, hid), BF16),
            shape((rows, hid), BF16),
        ),
        in_specs=[VMEM] * 5,
        out_specs=(VMEM, VMEM, VMEM),
        scratch_shapes=[
            pltpu.VMEM((hours, cells), F32),
            pltpu.VMEM((hours, cells), F32),
            pltpu.VMEM((attrs, cells), F32),
            pltpu.VMEM((hours, cells), F32),
            pltpu.VMEM((hours, cells), F32),
        ],
        compiler_params=pltpu.CompilerParams(vmem_limit_bytes=32 << 20),
        name="model",
    )(arrived, received_ct, w_in_v, w_hid_v, w_out_v)

    total = keep.astype(F32) + exchange(send, 0, 1).astype(F32)
    onehot = (inflow[0][:, None] == jnp.arange(reach_count, dtype=jnp.int32)[None, :]).astype(
        BF16
    )
    lateral = dot(runoff, onehot) * lateral_scale
    discharge = dot_high(lateral, inverse)
    bits = [(1 << b, 0) for b in range(regions.bit_length() - 1)]
    bits += [(0, 1 << b) for b in range(1, owners.bit_length() - 1)]
    stages = [bits[k : k + 2] for k in range(0, len(bits), 2)]
    if regions != 2:
        for _ in range(regions - 1):
            incoming = shifted(discharge, "region", 1)
            discharge = dot_high(lateral + dot_high(incoming, coupling), inverse)
    for stage, pair in enumerate(stages):
        block = lax.optimization_barrier(total.astype(BF16))
        bundle = block
        if stage == 0 and regions == 2:
            upper = lax.reduce_precision(discharge, 8, 7)
            bundle = jnp.concatenate(
                [block, upper.astype(BF16), (discharge - upper).astype(BF16)], axis=0
            )
        first = exchange(bundle, *pair[0])
        parts = [block, first[:rows]]
        if len(pair) == 2:
            (r0, c0), (r1, c1) = pair
            parts += [exchange(block, r1, c1), exchange(block, r0 ^ r1, c0 ^ c1)]
        parts = [p.astype(F32) for p in parts]
        total = parts[0] + parts[1]
        if len(pair) == 2:
            total = total + (parts[2] + parts[3])
        if stage == 0 and regions == 2:
            upper, lower = first[rows : rows + hours], first[rows + hours :]
            incoming = upper.astype(F32) + lower.astype(F32)
            incoming = jnp.where(lax.axis_index("region") == 0, 0.0, incoming)
            discharge = dot_high(lateral + dot_high(incoming, coupling), inverse)
    other = exchange(total, 0, 1)

    grad_in, grad_hid, grad_out = pl.pallas_call(
        functools.partial(finish_kernel, 1.0 / (regions * owners)),
        out_shape=(
            shape((attrs, hid), F32),
            shape((2, hid, hid), F32),
            shape((params, hid), F32),
        ),
        in_specs=[VMEM, VMEM],
        out_specs=(VMEM, VMEM, VMEM),
        compiler_params=pltpu.CompilerParams(vmem_limit_bytes=4 << 20),
        name="finish",
    )(total, other)
    return discharge, grad_in, grad_hid, grad_out.T


def solution(mesh):
    split = ("region", "cells")
    placed = (
        P(None, split),
        P(None, split),
        P(None, split),
        P(split),
        P(),
        P(),
        P(),
        P(split, None),
        P(split, None),
        P(None, split),
    )
    return jax.shard_map(
        per_device,
        mesh=mesh,
        in_specs=placed,
        out_specs=(P(None, split), P(), P(), P()),
        check_vma=False,
    )
```

```python
import functools

import jax
import jax.numpy as jnp
from jax import lax
from jax.experimental import pallas as pl
from jax.experimental.pallas import tpu as pltpu
from jax.sharding import PartitionSpec as P

F32 = jnp.float32
BF16 = jnp.bfloat16
LANES = 128
VMEM = pl.BlockSpec(memory_space=pltpu.VMEM)
HBM = pl.BlockSpec(memory_space=pltpu.HBM)
NT = (((1,), (1,)), ((), ()))
TN = (((0,), (0,)), ((), ()))


def dot(left, right, dims=(((1,), (0,)), ((), ()))):
    return lax.dot_general(left, right, dims, preferred_element_type=F32)


def dot_high(left, right, dims=(((1,), (0,)), ((), ()))):
    return lax.dot_general(
        left, right, dims, precision=lax.Precision.HIGHEST, preferred_element_type=F32
    )


def shifted(block, axis, distance):
    devices = range(lax.axis_size(axis))
    route = [(i - distance, i) for i in devices if i - distance in devices]
    return lax.ppermute(block, axis, route)


def swap_groups(group):
    lane = lax.broadcasted_iota(jnp.int32, group[0].shape, 1)
    half, quarter = LANES // 2, LANES // 4
    low = lane < half
    wide = [None] * 4
    for k in range(2):
        wide[k] = jnp.where(low, group[k], pltpu.roll(group[k + 2], half, 1))
        wide[k + 2] = jnp.where(low, pltpu.roll(group[k], half, 1), group[k + 2])
    even = lane % half < quarter
    out = [None] * 4
    for k in (0, 2):
        out[k] = jnp.where(even, wide[k], pltpu.roll(wide[k + 1], quarter, 1))
        out[k + 1] = jnp.where(even, pltpu.roll(wide[k], LANES - quarter, 1), wide[k + 1])
    return out


def open_kernel(
    attr_hbm,
    rain_hbm,
    demand_hbm,
    ct_hbm,
    inverse_hbm,
    coupling_hbm,
    inflow_hbm,
    w_in_hbm,
    w_hid_hbm,
    w_out_hbm,
    packed_ref,
    ct_ref,
    inverse_ref,
    coupling_ref,
    inflow_ref,
    w_in_ref,
    w_hid_ref,
    w_out_ref,
    attr_s,
    rain_s,
    demand_s,
    w_out_s,
    sems,
):
    pairs = [
        (rain_hbm, rain_s),
        (demand_hbm, demand_s),
        (attr_hbm, attr_s),
        (ct_hbm, ct_ref),
        (inverse_hbm, inverse_ref),
        (coupling_hbm, coupling_ref),
        (w_hid_hbm, w_hid_ref),
        (w_in_hbm, w_in_ref),
        (inflow_hbm, inflow_ref),
        (w_out_hbm, w_out_s),
    ]
    copies = [pltpu.make_async_copy(a, b, sems.at[i]) for i, (a, b) in enumerate(pairs)]
    for copy in copies:
        copy.start()
    hours, cells = rain_s.shape
    half = attr_s.shape[0] // 2
    for copy in copies[:3]:
        copy.wait()
    attr = attr_s[...].astype(F32)
    fill = jnp.zeros((hours - half, cells), F32)
    rows = [
        rain_s[...].astype(F32),
        demand_s[...].astype(F32),
        jnp.concatenate([attr[:half], fill], axis=0),
        jnp.concatenate([attr[half:], fill], axis=0),
    ]
    for column in range(cells // LANES):
        window = slice(column * LANES, (column + 1) * LANES)
        for k, block in enumerate(swap_groups([r[:, window] for r in rows])):
            packed_ref[4 * column + k] = block.astype(BF16)
    for copy in copies[3:]:
        copy.wait()
    out = w_out_s[...].astype(F32)
    wide = jnp.zeros((w_out_ref.shape[0] - out.shape[0], out.shape[1]), F32)
    w_out_ref[...] = jnp.concatenate([out, wide], axis=0).astype(BF16)


def cotangent_kernel(scale, start_ref, incoming_ref, inverse_ref, inflow_ref, received_ref):
    last = lax.axis_index("region") == lax.axis_size("region") - 1
    incoming = jnp.where(last, 0.0, incoming_ref[...])
    lateral_ct = start_ref[...] + dot_high(incoming, inverse_ref[...], NT)
    scaled = (lateral_ct * scale).astype(BF16)
    shape = (scaled.shape[1], inflow_ref.shape[1])
    onehot = (
        jnp.broadcast_to(inflow_ref[...], shape) == lax.broadcasted_iota(jnp.int32, shape, 0)
    ).astype(F32)
    received_ref[...] = dot(scaled, onehot.astype(BF16)).astype(BF16)


def main_kernel(
    packed_ref,
    ct_ref,
    w_in_ref,
    w_hid_ref,
    w_out_ref,
    runoff_ref,
    keep_ref,
    send_ref,
    rain_s,
    demand_s,
    attr_s,
    x_s,
    carry_s,
):
    hours, cells = rain_s.shape
    half = attr_s.shape[0] // 2
    for column in range(cells // LANES):
        window = slice(column * LANES, (column + 1) * LANES)
        rain, demand, first, second = swap_groups(
            [packed_ref[4 * column + k].astype(F32) for k in range(4)]
        )
        rain_s[:, window] = rain
        demand_s[:, window] = demand
        attr_s[:half, window] = first[:half]
        attr_s[half:, window] = second[:half]

    layers = w_hid_ref.shape[0]
    attr = attr_s[...].astype(BF16)
    wide = [jnp.tanh(dot(w_in_ref[...], attr, TN))]
    hidden = [wide[0].astype(BF16)]
    for layer in range(layers):
        wide.append(jnp.tanh(dot(w_hid_ref[layer], hidden[-1], TN)))
        hidden.append(wide[-1].astype(BF16))
    w_out = w_out_ref[...]
    params = dot(w_out, hidden[-1])[:8]
    gate = jax.nn.sigmoid(params)
    gate0, gate1, gate2, gate3 = (gate[i : i + 1] for i in range(4))
    drain = 0.02 + 0.3 * gate0
    capacity = 1.0 + 4.0 * gate1
    evap = 0.3 * gate2
    storage = gate3 * capacity

    demand = demand_s[...]
    kept = (1.0 - drain) - evap * demand
    carry_s[...] = kept
    rain_s[...] = rain_s[...] - capacity
    for hour in range(hours):
        x = storage + rain_s[hour : hour + 1]
        x_s[hour : hour + 1] = x
        under = jnp.maximum(-x, 0.0) + jnp.log(1.0 + jnp.exp(-jnp.abs(x)))
        storage = (capacity - under) * carry_s[hour : hour + 1]

    x = x_s[...]
    ct = ct_ref[...].astype(F32)
    small = jnp.exp(-jnp.abs(x))
    log = jnp.log(1.0 + small)
    spill = jnp.maximum(x, 0.0) + log
    level = capacity - (jnp.maximum(-x, 0.0) + log)
    runoff_ref[...] = (spill + drain * level).astype(BF16)
    share = 1.0 / (1.0 + small)
    slope = jnp.where(x >= 0.0, share, small * share)
    rest = 1.0 - slope
    x_s[...] = kept * rest
    rain_s[...] = ct * (drain * rest + slope)
    carry = jnp.zeros((1, cells), F32)
    for hour in range(hours - 1, -1, -1):
        carry_s[hour : hour + 1] = carry
        carry = carry * x_s[hour : hour + 1] + rain_s[hour : hour + 1]
    after = carry_s[...]
    level_ct = after * kept + ct * drain
    capacity_ct = -jnp.sum(slope * (ct - level_ct), axis=0, keepdims=True)
    held = after * level
    drain_ct = jnp.sum(level * ct - held, axis=0, keepdims=True)
    evap_ct = -jnp.sum(held * demand, axis=0, keepdims=True)
    capacity_ct = capacity_ct + carry * gate3
    params_ct = jnp.concatenate(
        [
            drain_ct * (0.3 * gate0 * (1.0 - gate0)),
            capacity_ct * (4.0 * gate1 * (1.0 - gate1)),
            evap_ct * (0.3 * gate2 * (1.0 - gate2)),
            carry * capacity * (gate3 * (1.0 - gate3)),
            jnp.zeros((w_out.shape[0] - 4, cells), F32),
        ],
        axis=0,
    ).astype(BF16)

    grad_out = dot(params_ct, hidden[-1], NT)
    back = dot(w_out, params_ct, TN)
    grads = [None] * layers
    for layer in range(layers - 1, -1, -1):
        top = wide[layer + 1]
        g = (back * (1.0 - top * top)).astype(BF16)
        grads[layer] = dot(hidden[layer], g, NT)
        back = dot(w_hid_ref[layer], g)
    g = (back * (1.0 - wide[0] * wide[0])).astype(BF16)
    grad_in = dot(attr, g, NT)

    rows, width = keep_ref.shape
    fill = rows - grads[1].shape[0] - grad_out.shape[0]
    first = jnp.concatenate([grads[0], grad_in], axis=0)
    second = jnp.concatenate([grads[1], grad_out, jnp.zeros((fill, width), F32)], axis=0)
    lower = lax.axis_index("cells") & 1 == 0

    @pl.when(lower)
    def _():
        keep_ref[...] = first.astype(BF16)
        send_ref[...] = second.astype(BF16)

    @pl.when(jnp.logical_not(lower))
    def _():
        keep_ref[...] = second.astype(BF16)
        send_ref[...] = first.astype(BF16)


def finish_kernel(scale, mine_ref, other_ref, grad_in_ref, grad_hid_ref, grad_out_ref):
    hid = grad_hid_ref.shape[1]
    params = grad_out_ref.shape[0]

    def place(first, second):
        grad_hid_ref[0] = first[:hid] * scale
        grad_in_ref[...] = first[hid:] * scale
        grad_hid_ref[1] = second[:hid] * scale
        grad_out_ref[...] = second[hid : hid + params] * scale

    lower = lax.axis_index("cells") & 1 == 0

    @pl.when(lower)
    def _():
        place(mine_ref, other_ref)

    @pl.when(jnp.logical_not(lower))
    def _():
        place(other_ref, mine_ref)


def exchange(block, region_flip, cells_flip):
    regions, cells = lax.axis_size("region"), lax.axis_size("cells")
    route = [
        (r * cells + c, (r ^ region_flip) * cells + (c ^ cells_flip))
        for r in range(regions)
        for c in range(cells)
    ]
    return lax.ppermute(block, ("region", "cells"), route)


def per_device(
    attributes,
    precip,
    pet_demand,
    inflow_reach,
    w_in,
    w_hid,
    w_out,
    block_inverse,
    upstream_coupling,
    discharge_cotangent,
):
    hours, cells = precip.shape
    regions, owners = lax.axis_size("region"), lax.axis_size("cells")
    attrs, hid = w_in.shape
    params = w_out.shape[1]
    reach_count = block_inverse.shape[1]
    lateral_scale = reach_count / cells
    assert 4 * cells == LANES * owners and w_hid.shape[0] == 2
    assert regions & (regions - 1) == 0 and owners & (owners - 1) == 0
    shape = jax.ShapeDtypeStruct

    def in_hbm(array):
        return pltpu.with_memory_space_constraint(array, pltpu.HBM)

    packed, ct, inverse, coupling, inflow, w_in_v, w_hid_v, w_out_v = pl.pallas_call(
        open_kernel,
        out_shape=(
            pltpu.VMEM((owners, hours, LANES), BF16),
            shape((hours, reach_count), F32),
            shape(block_inverse.shape, F32),
            shape(upstream_coupling.shape, F32),
            shape((1, cells), jnp.int32),
            shape(w_in.shape, BF16),
            shape(w_hid.shape, BF16),
            shape((16, hid), BF16),
        ),
        in_specs=[HBM] * 10,
        out_specs=(VMEM,) * 8,
        scratch_shapes=[
            pltpu.VMEM((attrs, cells), BF16),
            pltpu.VMEM((hours, cells), BF16),
            pltpu.VMEM((hours, cells), BF16),
            pltpu.VMEM((params, hid), BF16),
            pltpu.SemaphoreType.DMA((10,)),
        ],
        compiler_params=pltpu.CompilerParams(vmem_limit_bytes=8 << 20),
        name="open",
    )(
        in_hbm(attributes),
        in_hbm(precip),
        in_hbm(pet_demand),
        in_hbm(discharge_cotangent),
        in_hbm(block_inverse),
        in_hbm(upstream_coupling),
        in_hbm(inflow_reach.reshape(1, cells)),
        in_hbm(w_in),
        in_hbm(w_hid),
        in_hbm(w_out.T),
    )
    arrived = lax.all_to_all(packed, "cells", split_axis=0, concat_axis=0, tiled=True)

    start_ct = dot_high(ct, inverse, NT)
    outgoing = dot_high(start_ct, coupling, NT)
    incoming = jnp.zeros_like(start_ct)
    for step in range(regions - 1):
        if step:
            lateral_ct = start_ct + dot_high(incoming, inverse, NT)
            outgoing = dot_high(lateral_ct, coupling, NT)
        if regions == 2:
            incoming = exchange(outgoing, 1, 0)
        else:
            incoming = shifted(outgoing, "region", -1)
    received_ct = pl.pallas_call(
        functools.partial(cotangent_kernel, lateral_scale),
        out_shape=shape((hours, cells), BF16),
        in_specs=[VMEM] * 4,
        out_specs=VMEM,
        compiler_params=pltpu.CompilerParams(vmem_limit_bytes=8 << 20),
        name="cotangent",
    )(start_ct, incoming, inverse, inflow)

    rows = hid + attrs
    runoff, keep, send = pl.pallas_call(
        main_kernel,
        out_shape=(
            shape((hours, cells), BF16),
            shape((rows, hid), BF16),
            shape((rows, hid), BF16),
        ),
        in_specs=[VMEM] * 5,
        out_specs=(VMEM, VMEM, VMEM),
        scratch_shapes=[
            pltpu.VMEM((hours, cells), F32),
            pltpu.VMEM((hours, cells), F32),
            pltpu.VMEM((attrs, cells), F32),
            pltpu.VMEM((hours, cells), F32),
            pltpu.VMEM((hours, cells), F32),
        ],
        compiler_params=pltpu.CompilerParams(vmem_limit_bytes=32 << 20),
        name="model",
    )(arrived, received_ct, w_in_v, w_hid_v, w_out_v)

    total = keep.astype(F32) + exchange(send, 0, 1).astype(F32)
    onehot = (inflow[0][:, None] == jnp.arange(reach_count, dtype=jnp.int32)[None, :]).astype(
        BF16
    )
    lateral = dot(runoff, onehot) * lateral_scale
    discharge = dot_high(lateral, inverse)
    bits = [(1 << b, 0) for b in range(regions.bit_length() - 1)]
    bits += [(0, 1 << b) for b in range(1, owners.bit_length() - 1)]
    stages = [bits[k : k + 2] for k in range(0, len(bits), 2)]
    if regions != 2:
        for _ in range(regions - 1):
            incoming = shifted(discharge, "region", 1)
            discharge = dot_high(lateral + dot_high(incoming, coupling), inverse)
    for stage, pair in enumerate(stages):
        block = lax.optimization_barrier(total.astype(BF16))
        bundle = block
        if stage == 0 and regions == 2:
            upper = lax.reduce_precision(discharge, 8, 7)
            bundle = jnp.concatenate(
                [block, upper.astype(BF16), (discharge - upper).astype(BF16)], axis=0
            )
        first = exchange(bundle, *pair[0])
        parts = [block, first[:rows]]
        if len(pair) == 2:
            (r0, c0), (r1, c1) = pair
            parts += [exchange(block, r1, c1), exchange(block, r0 ^ r1, c0 ^ c1)]
        parts = [p.astype(F32) for p in parts]
        total = parts[0] + parts[1]
        if len(pair) == 2:
            total = total + (parts[2] + parts[3])
        if stage == 0 and regions == 2:
            upper, lower = first[rows : rows + hours], first[rows + hours :]
            incoming = upper.astype(F32) + lower.astype(F32)
            incoming = jnp.where(lax.axis_index("region") == 0, 0.0, incoming)
            discharge = dot_high(lateral + dot_high(incoming, coupling), inverse)
    other = exchange(total, 0, 1)

    grad_in, grad_hid, grad_out = pl.pallas_call(
        functools.partial(finish_kernel, 1.0 / (regions * owners)),
        out_shape=(
            shape((attrs, hid), F32),
            shape((2, hid, hid), F32),
            shape((params, hid), F32),
        ),
        in_specs=[VMEM, VMEM],
        out_specs=(VMEM, VMEM, VMEM),
        compiler_params=pltpu.CompilerParams(vmem_limit_bytes=4 << 20),
        name="finish",
    )(total, other)
    return discharge, grad_in, grad_hid, grad_out.T


def solution(mesh):
    split = ("region", "cells")
    placed = (
        P(None, split),
        P(None, split),
        P(None, split),
        P(split),
        P(),
        P(),
        P(),
        P(split, None),
        P(split, None),
        P(None, split),
    )
    return jax.shard_map(
        per_device,
        mesh=mesh,
        in_specs=placed,
        out_specs=(P(None, split), P(), P(), P()),
        check_vma=False,
    )
```

```python
import functools

import jax
import jax.numpy as jnp
from jax import lax
from jax.experimental import pallas as pl
from jax.experimental.pallas import tpu as pltpu
from jax.sharding import PartitionSpec as P

F32 = jnp.float32
BF16 = jnp.bfloat16
LANES = 128
VMEM = pl.BlockSpec(memory_space=pltpu.VMEM)
HBM = pl.BlockSpec(memory_space=pltpu.HBM)
NT = (((1,), (1,)), ((), ()))
TN = (((0,), (0,)), ((), ()))


def dot(left, right, dims=(((1,), (0,)), ((), ()))):
    return lax.dot_general(left, right, dims, preferred_element_type=F32)


def dot_high(left, right, dims=(((1,), (0,)), ((), ()))):
    return lax.dot_general(
        left, right, dims, precision=lax.Precision.HIGHEST, preferred_element_type=F32
    )


def shifted(block, axis, distance):
    devices = range(lax.axis_size(axis))
    route = [(i - distance, i) for i in devices if i - distance in devices]
    return lax.ppermute(block, axis, route)


def place(device, devices):
    return (devices // 2 - 1 - device) % devices


def swap_groups(group):
    lane = lax.broadcasted_iota(jnp.int32, group[0].shape, 1)
    half, quarter = LANES // 2, LANES // 4
    low = lane < half
    wide = [None] * 4
    for k in range(2):
        wide[k] = jnp.where(low, group[k], pltpu.roll(group[k + 2], half, 1))
        wide[k + 2] = jnp.where(low, pltpu.roll(group[k], half, 1), group[k + 2])
    even = lane % half < quarter
    out = [None] * 4
    for k in (0, 2):
        out[k] = jnp.where(even, wide[k], pltpu.roll(wide[k + 1], quarter, 1))
        out[k + 1] = jnp.where(even, pltpu.roll(wide[k], LANES - quarter, 1), wide[k + 1])
    return out


def open_kernel(
    attr_hbm,
    rain_hbm,
    demand_hbm,
    ct_hbm,
    inverse_hbm,
    coupling_hbm,
    inflow_hbm,
    w_in_hbm,
    w_hid_hbm,
    w_out_hbm,
    packed_ref,
    ct_ref,
    inverse_ref,
    coupling_ref,
    inflow_ref,
    w_in_ref,
    w_hid_ref,
    w_out_ref,
    attr_s,
    rain_s,
    demand_s,
    w_out_s,
    sems,
):
    pairs = [
        (rain_hbm, rain_s),
        (demand_hbm, demand_s),
        (attr_hbm, attr_s),
        (ct_hbm, ct_ref),
        (inverse_hbm, inverse_ref),
        (coupling_hbm, coupling_ref),
        (w_hid_hbm, w_hid_ref),
        (w_in_hbm, w_in_ref),
        (inflow_hbm, inflow_ref),
        (w_out_hbm, w_out_s),
    ]
    copies = [pltpu.make_async_copy(a, b, sems.at[i]) for i, (a, b) in enumerate(pairs)]
    for copy in copies:
        copy.start()
    hours, cells = rain_s.shape
    half = attr_s.shape[0] // 2
    for copy in copies[:3]:
        copy.wait()
    attr = attr_s[...].astype(F32)
    fill = jnp.zeros((hours - half, cells), F32)
    rows = [
        rain_s[...].astype(F32),
        demand_s[...].astype(F32),
        jnp.concatenate([attr[:half], fill], axis=0),
        jnp.concatenate([attr[half:], fill], axis=0),
    ]
    for column in range(cells // LANES):
        window = slice(column * LANES, (column + 1) * LANES)
        for k, block in enumerate(swap_groups([r[:, window] for r in rows])):
            packed_ref[place(4 * column + k, packed_ref.shape[0])] = block.astype(BF16)
    for copy in copies[3:]:
        copy.wait()
    out = w_out_s[...].astype(F32)
    wide = jnp.zeros((w_out_ref.shape[0] - out.shape[0], out.shape[1]), F32)
    w_out_ref[...] = jnp.concatenate([out, wide], axis=0).astype(BF16)


def cotangent_kernel(scale, start_ref, incoming_ref, inverse_ref, inflow_ref, received_ref):
    last = lax.axis_index("region") == lax.axis_size("region") - 1
    incoming = jnp.where(last, 0.0, incoming_ref[...])
    lateral_ct = start_ref[...] + dot_high(incoming, inverse_ref[...], NT)
    scaled = (lateral_ct * scale).astype(BF16)
    shape = (scaled.shape[1], inflow_ref.shape[1])
    onehot = (
        jnp.broadcast_to(inflow_ref[...], shape) == lax.broadcasted_iota(jnp.int32, shape, 0)
    ).astype(F32)
    received_ref[...] = dot(scaled, onehot.astype(BF16)).astype(BF16)


def main_kernel(
    packed_ref,
    ct_ref,
    w_in_ref,
    w_hid_ref,
    w_out_ref,
    runoff_ref,
    keep_ref,
    send_ref,
    rain_s,
    demand_s,
    attr_s,
    x_s,
    carry_s,
):
    hours, cells = rain_s.shape
    half = attr_s.shape[0] // 2
    for column in range(cells // LANES):
        window = slice(column * LANES, (column + 1) * LANES)
        rain, demand, first, second = swap_groups(
            [
                packed_ref[place(4 * column + k, packed_ref.shape[0])].astype(F32)
                for k in range(4)
            ]
        )
        rain_s[:, window] = rain
        demand_s[:, window] = demand
        attr_s[:half, window] = first[:half]
        attr_s[half:, window] = second[:half]

    layers = w_hid_ref.shape[0]
    attr = attr_s[...].astype(BF16)
    wide = [jnp.tanh(dot(w_in_ref[...], attr, TN))]
    hidden = [wide[0].astype(BF16)]
    for layer in range(layers):
        wide.append(jnp.tanh(dot(w_hid_ref[layer], hidden[-1], TN)))
        hidden.append(wide[-1].astype(BF16))
    w_out = w_out_ref[...]
    params = dot(w_out, hidden[-1])[:8]
    gate = jax.nn.sigmoid(params)
    gate0, gate1, gate2, gate3 = (gate[i : i + 1] for i in range(4))
    drain = 0.02 + 0.3 * gate0
    capacity = 1.0 + 4.0 * gate1
    evap = 0.3 * gate2
    storage = gate3 * capacity

    demand = demand_s[...]
    kept = (1.0 - drain) - evap * demand
    carry_s[...] = kept
    rain_s[...] = rain_s[...] - capacity
    for hour in range(hours):
        x = storage + rain_s[hour : hour + 1]
        x_s[hour : hour + 1] = x
        under = jnp.maximum(-x, 0.0) + jnp.log(1.0 + jnp.exp(-jnp.abs(x)))
        storage = (capacity - under) * carry_s[hour : hour + 1]

    x = x_s[...]
    ct = ct_ref[...].astype(F32)
    small = jnp.exp(-jnp.abs(x))
    log = jnp.log(1.0 + small)
    spill = jnp.maximum(x, 0.0) + log
    level = capacity - (jnp.maximum(-x, 0.0) + log)
    runoff_ref[...] = (spill + drain * level).astype(BF16)
    share = 1.0 / (1.0 + small)
    slope = jnp.where(x >= 0.0, share, small * share)
    rest = 1.0 - slope
    x_s[...] = kept * rest
    rain_s[...] = ct * (drain * rest + slope)
    carry = jnp.zeros((1, cells), F32)
    for hour in range(hours - 1, -1, -1):
        carry_s[hour : hour + 1] = carry
        carry = carry * x_s[hour : hour + 1] + rain_s[hour : hour + 1]
    after = carry_s[...]
    level_ct = after * kept + ct * drain
    capacity_ct = -jnp.sum(slope * (ct - level_ct), axis=0, keepdims=True)
    held = after * level
    drain_ct = jnp.sum(level * ct - held, axis=0, keepdims=True)
    evap_ct = -jnp.sum(held * demand, axis=0, keepdims=True)
    capacity_ct = capacity_ct + carry * gate3
    params_ct = jnp.concatenate(
        [
            drain_ct * (0.3 * gate0 * (1.0 - gate0)),
            capacity_ct * (4.0 * gate1 * (1.0 - gate1)),
            evap_ct * (0.3 * gate2 * (1.0 - gate2)),
            carry * capacity * (gate3 * (1.0 - gate3)),
            jnp.zeros((w_out.shape[0] - 4, cells), F32),
        ],
        axis=0,
    ).astype(BF16)

    grad_out = dot(params_ct, hidden[-1], NT)
    back = dot(w_out, params_ct, TN)
    grads = [None] * layers
    for layer in range(layers - 1, -1, -1):
        top = wide[layer + 1]
        g = (back * (1.0 - top * top)).astype(BF16)
        grads[layer] = dot(hidden[layer], g, NT)
        back = dot(w_hid_ref[layer], g)
    g = (back * (1.0 - wide[0] * wide[0])).astype(BF16)
    grad_in = dot(attr, g, NT)

    rows, width = keep_ref.shape
    fill = rows - grads[1].shape[0] - grad_out.shape[0]
    first = jnp.concatenate([grads[0], grad_in], axis=0)
    second = jnp.concatenate([grads[1], grad_out, jnp.zeros((fill, width), F32)], axis=0)
    lower = lax.axis_index("cells") & 1 == 0

    @pl.when(lower)
    def _():
        keep_ref[...] = first.astype(BF16)
        send_ref[...] = second.astype(BF16)

    @pl.when(jnp.logical_not(lower))
    def _():
        keep_ref[...] = second.astype(BF16)
        send_ref[...] = first.astype(BF16)


def finish_kernel(scale, mine_ref, other_ref, grad_in_ref, grad_hid_ref, grad_out_ref):
    hid = grad_hid_ref.shape[1]
    params = grad_out_ref.shape[0]

    def place(first, second):
        grad_hid_ref[0] = first[:hid] * scale
        grad_in_ref[...] = first[hid:] * scale
        grad_hid_ref[1] = second[:hid] * scale
        grad_out_ref[...] = second[hid : hid + params] * scale

    lower = lax.axis_index("cells") & 1 == 0

    @pl.when(lower)
    def _():
        place(mine_ref, other_ref)

    @pl.when(jnp.logical_not(lower))
    def _():
        place(other_ref, mine_ref)


def exchange(block, region_flip, cells_flip):
    regions, cells = lax.axis_size("region"), lax.axis_size("cells")
    route = [
        (r * cells + c, (r ^ region_flip) * cells + (c ^ cells_flip))
        for r in range(regions)
        for c in range(cells)
    ]
    return lax.ppermute(block, ("region", "cells"), route)


def per_device(
    attributes,
    precip,
    pet_demand,
    inflow_reach,
    w_in,
    w_hid,
    w_out,
    block_inverse,
    upstream_coupling,
    discharge_cotangent,
):
    hours, cells = precip.shape
    regions, owners = lax.axis_size("region"), lax.axis_size("cells")
    attrs, hid = w_in.shape
    params = w_out.shape[1]
    reach_count = block_inverse.shape[1]
    lateral_scale = reach_count / cells
    assert 4 * cells == LANES * owners and w_hid.shape[0] == 2
    assert regions & (regions - 1) == 0 and owners & (owners - 1) == 0
    shape = jax.ShapeDtypeStruct

    def in_hbm(array):
        return pltpu.with_memory_space_constraint(array, pltpu.HBM)

    packed, ct, inverse, coupling, inflow, w_in_v, w_hid_v, w_out_v = pl.pallas_call(
        open_kernel,
        out_shape=(
            pltpu.VMEM((owners, hours, LANES), BF16),
            shape((hours, reach_count), F32),
            shape(block_inverse.shape, F32),
            shape(upstream_coupling.shape, F32),
            shape((1, cells), jnp.int32),
            shape(w_in.shape, BF16),
            shape(w_hid.shape, BF16),
            shape((16, hid), BF16),
        ),
        in_specs=[HBM] * 10,
        out_specs=(VMEM,) * 8,
        scratch_shapes=[
            pltpu.VMEM((attrs, cells), BF16),
            pltpu.VMEM((hours, cells), BF16),
            pltpu.VMEM((hours, cells), BF16),
            pltpu.VMEM((params, hid), BF16),
            pltpu.SemaphoreType.DMA((10,)),
        ],
        compiler_params=pltpu.CompilerParams(vmem_limit_bytes=8 << 20),
        name="open",
    )(
        in_hbm(attributes),
        in_hbm(precip),
        in_hbm(pet_demand),
        in_hbm(discharge_cotangent),
        in_hbm(block_inverse),
        in_hbm(upstream_coupling),
        in_hbm(inflow_reach.reshape(1, cells)),
        in_hbm(w_in),
        in_hbm(w_hid),
        in_hbm(w_out.T),
    )
    arrived = lax.all_to_all(
        packed,
        "cells",
        split_axis=0,
        concat_axis=0,
        tiled=True,
        axis_index_groups=[[place(k, owners) for k in range(owners)]],
    )

    start_ct = dot_high(ct, inverse, NT)
    outgoing = dot_high(start_ct, coupling, NT)
    incoming = jnp.zeros_like(start_ct)
    for step in range(regions - 1):
        if step:
            lateral_ct = start_ct + dot_high(incoming, inverse, NT)
            outgoing = dot_high(lateral_ct, coupling, NT)
        if regions == 2:
            incoming = exchange(outgoing, 1, 0)
        else:
            incoming = shifted(outgoing, "region", -1)
    received_ct = pl.pallas_call(
        functools.partial(cotangent_kernel, lateral_scale),
        out_shape=shape((hours, cells), BF16),
        in_specs=[VMEM] * 4,
        out_specs=VMEM,
        compiler_params=pltpu.CompilerParams(vmem_limit_bytes=8 << 20),
        name="cotangent",
    )(start_ct, incoming, inverse, inflow)

    rows = hid + attrs
    runoff, keep, send = pl.pallas_call(
        main_kernel,
        out_shape=(
            shape((hours, cells), BF16),
            shape((rows, hid), BF16),
            shape((rows, hid), BF16),
        ),
        in_specs=[VMEM] * 5,
        out_specs=(VMEM, VMEM, VMEM),
        scratch_shapes=[
            pltpu.VMEM((hours, cells), F32),
            pltpu.VMEM((hours, cells), F32),
            pltpu.VMEM((attrs, cells), F32),
            pltpu.VMEM((hours, cells), F32),
            pltpu.VMEM((hours, cells), F32),
        ],
        compiler_params=pltpu.CompilerParams(vmem_limit_bytes=32 << 20),
        name="model",
    )(arrived, received_ct, w_in_v, w_hid_v, w_out_v)

    total = keep.astype(F32) + exchange(send, 0, 1).astype(F32)
    onehot = (inflow[0][:, None] == jnp.arange(reach_count, dtype=jnp.int32)[None, :]).astype(
        BF16
    )
    lateral = dot(runoff, onehot) * lateral_scale
    discharge = dot_high(lateral, inverse)
    bits = [(1 << b, 0) for b in range(regions.bit_length() - 1)]
    bits += [(0, 1 << b) for b in range(1, owners.bit_length() - 1)]
    stages = [bits[k : k + 2] for k in range(0, len(bits), 2)]
    if regions != 2:
        for _ in range(regions - 1):
            incoming = shifted(discharge, "region", 1)
            discharge = dot_high(lateral + dot_high(incoming, coupling), inverse)
    for stage, pair in enumerate(stages):
        block = lax.optimization_barrier(total.astype(BF16))
        bundle = block
        if stage == 0 and regions == 2:
            upper = lax.reduce_precision(discharge, 8, 7)
            bundle = jnp.concatenate(
                [block, upper.astype(BF16), (discharge - upper).astype(BF16)], axis=0
            )
        first = exchange(bundle, *pair[0])
        parts = [block, first[:rows]]
        if len(pair) == 2:
            (r0, c0), (r1, c1) = pair
            parts += [exchange(block, r1, c1), exchange(block, r0 ^ r1, c0 ^ c1)]
        parts = [p.astype(F32) for p in parts]
        total = parts[0] + parts[1]
        if len(pair) == 2:
            total = total + (parts[2] + parts[3])
        if stage == 0 and regions == 2:
            upper, lower = first[rows : rows + hours], first[rows + hours :]
            incoming = upper.astype(F32) + lower.astype(F32)
            incoming = jnp.where(lax.axis_index("region") == 0, 0.0, incoming)
            discharge = dot_high(lateral + dot_high(incoming, coupling), inverse)
    other = exchange(total, 0, 1)

    grad_in, grad_hid, grad_out = pl.pallas_call(
        functools.partial(finish_kernel, 1.0 / (regions * owners)),
        out_shape=(
            shape((attrs, hid), F32),
            shape((2, hid, hid), F32),
            shape((params, hid), F32),
        ),
        in_specs=[VMEM, VMEM],
        out_specs=(VMEM, VMEM, VMEM),
        compiler_params=pltpu.CompilerParams(vmem_limit_bytes=4 << 20),
        name="finish",
    )(total, other)
    return discharge, grad_in, grad_hid, grad_out.T


def solution(mesh):
    split = ("region", "cells")
    placed = (
        P(None, split),
        P(None, split),
        P(None, split),
        P(split),
        P(),
        P(),
        P(),
        P(split, None),
        P(split, None),
        P(None, split),
    )
    return jax.shard_map(
        per_device,
        mesh=mesh,
        in_specs=placed,
        out_specs=(P(None, split), P(), P(), P()),
        check_vma=False,
    )
```

```python
import functools

import jax
import jax.numpy as jnp
from jax import lax
from jax.experimental import pallas as pl
from jax.experimental.pallas import tpu as pltpu
from jax.sharding import PartitionSpec as P

F32 = jnp.float32
BF16 = jnp.bfloat16
LANES = 128
VMEM = pl.BlockSpec(memory_space=pltpu.VMEM)
HBM = pl.BlockSpec(memory_space=pltpu.HBM)
NT = (((1,), (1,)), ((), ()))
TN = (((0,), (0,)), ((), ()))


def dot(left, right, dims=(((1,), (0,)), ((), ()))):
    return lax.dot_general(left, right, dims, preferred_element_type=F32)


def dot_high(left, right, dims=(((1,), (0,)), ((), ()))):
    return lax.dot_general(
        left, right, dims, precision=lax.Precision.HIGHEST, preferred_element_type=F32
    )


def shifted(block, axis, distance):
    devices = range(lax.axis_size(axis))
    route = [(i - distance, i) for i in devices if i - distance in devices]
    return lax.ppermute(block, axis, route)


def place(device, devices):
    return device ^ (devices // 2 + 3)


def swap_groups(group):
    lane = lax.broadcasted_iota(jnp.int32, group[0].shape, 1)
    half, quarter = LANES // 2, LANES // 4
    low = lane < half
    wide = [None] * 4
    for k in range(2):
        wide[k] = jnp.where(low, group[k], pltpu.roll(group[k + 2], half, 1))
        wide[k + 2] = jnp.where(low, pltpu.roll(group[k], half, 1), group[k + 2])
    even = lane % half < quarter
    out = [None] * 4
    for k in (0, 2):
        out[k] = jnp.where(even, wide[k], pltpu.roll(wide[k + 1], quarter, 1))
        out[k + 1] = jnp.where(even, pltpu.roll(wide[k], LANES - quarter, 1), wide[k + 1])
    return out


def open_kernel(
    attr_hbm,
    rain_hbm,
    demand_hbm,
    ct_hbm,
    inverse_hbm,
    coupling_hbm,
    inflow_hbm,
    w_in_hbm,
    w_hid_hbm,
    w_out_hbm,
    packed_ref,
    ct_ref,
    inverse_ref,
    coupling_ref,
    inflow_ref,
    w_in_ref,
    w_hid_ref,
    w_out_ref,
    attr_s,
    rain_s,
    demand_s,
    w_out_s,
    sems,
):
    pairs = [
        (rain_hbm, rain_s),
        (demand_hbm, demand_s),
        (attr_hbm, attr_s),
        (ct_hbm, ct_ref),
        (inverse_hbm, inverse_ref),
        (coupling_hbm, coupling_ref),
        (w_hid_hbm, w_hid_ref),
        (w_in_hbm, w_in_ref),
        (inflow_hbm, inflow_ref),
        (w_out_hbm, w_out_s),
    ]
    copies = [pltpu.make_async_copy(a, b, sems.at[i]) for i, (a, b) in enumerate(pairs)]
    for copy in copies:
        copy.start()
    hours, cells = rain_s.shape
    half = attr_s.shape[0] // 2
    for copy in copies[:3]:
        copy.wait()
    attr = attr_s[...].astype(F32)
    fill = jnp.zeros((hours - half, cells), F32)
    rows = [
        rain_s[...].astype(F32),
        demand_s[...].astype(F32),
        jnp.concatenate([attr[:half], fill], axis=0),
        jnp.concatenate([attr[half:], fill], axis=0),
    ]
    for column in range(cells // LANES):
        window = slice(column * LANES, (column + 1) * LANES)
        for k, block in enumerate(swap_groups([r[:, window] for r in rows])):
            packed_ref[place(4 * column + k, packed_ref.shape[0])] = block.astype(BF16)
    for copy in copies[3:]:
        copy.wait()
    out = w_out_s[...].astype(F32)
    wide = jnp.zeros((w_out_ref.shape[0] - out.shape[0], out.shape[1]), F32)
    w_out_ref[...] = jnp.concatenate([out, wide], axis=0).astype(BF16)


def received_cotangent(scale, start_ref, incoming_ref, inverse_ref, inflow_ref):
    last = lax.axis_index("region") == lax.axis_size("region") - 1
    incoming = jnp.where(last, 0.0, incoming_ref[...])
    lateral_ct = start_ref[...] + dot_high(incoming, inverse_ref[...], NT)
    scaled = (lateral_ct * scale).astype(BF16)
    shape = (scaled.shape[1], inflow_ref.shape[1])
    onehot = (
        jnp.broadcast_to(inflow_ref[...], shape) == lax.broadcasted_iota(jnp.int32, shape, 0)
    ).astype(F32)
    return dot(scaled, onehot.astype(BF16)).astype(BF16).astype(F32)


def main_kernel(
    scale,
    packed_ref,
    start_ref,
    incoming_ref,
    inverse_ref,
    inflow_ref,
    w_in_ref,
    w_hid_ref,
    w_out_ref,
    runoff_ref,
    keep_ref,
    send_ref,
    rain_s,
    demand_s,
    attr_s,
    x_s,
    carry_s,
):
    hours, cells = rain_s.shape
    half = attr_s.shape[0] // 2
    for column in range(cells // LANES):
        window = slice(column * LANES, (column + 1) * LANES)
        rain, demand, first, second = swap_groups(
            [
                packed_ref[place(4 * column + k, packed_ref.shape[0])].astype(F32)
                for k in range(4)
            ]
        )
        rain_s[:, window] = rain
        demand_s[:, window] = demand
        attr_s[:half, window] = first[:half]
        attr_s[half:, window] = second[:half]

    layers = w_hid_ref.shape[0]
    attr = attr_s[...].astype(BF16)
    wide = [jnp.tanh(dot(w_in_ref[...], attr, TN))]
    hidden = [wide[0].astype(BF16)]
    for layer in range(layers):
        wide.append(jnp.tanh(dot(w_hid_ref[layer], hidden[-1], TN)))
        hidden.append(wide[-1].astype(BF16))
    w_out = w_out_ref[...]
    params = dot(w_out, hidden[-1])[:8]
    gate = jax.nn.sigmoid(params)
    gate0, gate1, gate2, gate3 = (gate[i : i + 1] for i in range(4))
    drain = 0.02 + 0.3 * gate0
    capacity = 1.0 + 4.0 * gate1
    evap = 0.3 * gate2
    storage = gate3 * capacity

    demand = demand_s[...]
    kept = (1.0 - drain) - evap * demand
    carry_s[...] = kept
    rain_s[...] = rain_s[...] - capacity
    for hour in range(hours):
        x = storage + rain_s[hour : hour + 1]
        x_s[hour : hour + 1] = x
        under = jnp.maximum(-x, 0.0) + jnp.log(1.0 + jnp.exp(-jnp.abs(x)))
        storage = (capacity - under) * carry_s[hour : hour + 1]

    x = x_s[...]
    ct = received_cotangent(scale, start_ref, incoming_ref, inverse_ref, inflow_ref)
    small = jnp.exp(-jnp.abs(x))
    log = jnp.log(1.0 + small)
    spill = jnp.maximum(x, 0.0) + log
    level = capacity - (jnp.maximum(-x, 0.0) + log)
    runoff_ref[...] = (spill + drain * level).astype(BF16)
    share = 1.0 / (1.0 + small)
    slope = jnp.where(x >= 0.0, share, small * share)
    rest = 1.0 - slope
    x_s[...] = kept * rest
    rain_s[...] = ct * (drain * rest + slope)
    carry = jnp.zeros((1, cells), F32)
    for hour in range(hours - 1, -1, -1):
        carry_s[hour : hour + 1] = carry
        carry = carry * x_s[hour : hour + 1] + rain_s[hour : hour + 1]
    after = carry_s[...]
    level_ct = after * kept + ct * drain
    capacity_ct = -jnp.sum(slope * (ct - level_ct), axis=0, keepdims=True)
    held = after * level
    drain_ct = jnp.sum(level * ct - held, axis=0, keepdims=True)
    evap_ct = -jnp.sum(held * demand, axis=0, keepdims=True)
    capacity_ct = capacity_ct + carry * gate3
    params_ct = jnp.concatenate(
        [
            drain_ct * (0.3 * gate0 * (1.0 - gate0)),
            capacity_ct * (4.0 * gate1 * (1.0 - gate1)),
            evap_ct * (0.3 * gate2 * (1.0 - gate2)),
            carry * capacity * (gate3 * (1.0 - gate3)),
            jnp.zeros((w_out.shape[0] - 4, cells), F32),
        ],
        axis=0,
    ).astype(BF16)

    grad_out = dot(params_ct, hidden[-1], NT)
    back = dot(w_out, params_ct, TN)
    grads = [None] * layers
    for layer in range(layers - 1, -1, -1):
        top = wide[layer + 1]
        g = (back * (1.0 - top * top)).astype(BF16)
        grads[layer] = dot(hidden[layer], g, NT)
        back = dot(w_hid_ref[layer], g)
    g = (back * (1.0 - wide[0] * wide[0])).astype(BF16)
    grad_in = dot(attr, g, NT)

    rows, width = keep_ref.shape
    fill = rows - grads[1].shape[0] - grad_out.shape[0]
    first = jnp.concatenate([grads[0], grad_in], axis=0)
    second = jnp.concatenate([grads[1], grad_out, jnp.zeros((fill, width), F32)], axis=0)
    lower = lax.axis_index("cells") & 1 == 0

    @pl.when(lower)
    def _():
        keep_ref[...] = first.astype(BF16)
        send_ref[...] = second.astype(BF16)

    @pl.when(jnp.logical_not(lower))
    def _():
        keep_ref[...] = second.astype(BF16)
        send_ref[...] = first.astype(BF16)


def finish_kernel(scale, mine_ref, other_ref, grad_in_ref, grad_hid_ref, grad_out_ref):
    hid = grad_hid_ref.shape[1]
    params = grad_out_ref.shape[0]

    def place(first, second):
        grad_hid_ref[0] = first[:hid] * scale
        grad_in_ref[...] = first[hid:] * scale
        grad_hid_ref[1] = second[:hid] * scale
        grad_out_ref[...] = second[hid : hid + params] * scale

    lower = lax.axis_index("cells") & 1 == 0

    @pl.when(lower)
    def _():
        place(mine_ref, other_ref)

    @pl.when(jnp.logical_not(lower))
    def _():
        place(other_ref, mine_ref)


def exchange(block, region_flip, cells_flip):
    regions, cells = lax.axis_size("region"), lax.axis_size("cells")
    route = [
        (r * cells + c, (r ^ region_flip) * cells + (c ^ cells_flip))
        for r in range(regions)
        for c in range(cells)
    ]
    return lax.ppermute(block, ("region", "cells"), route)


def per_device(
    attributes,
    precip,
    pet_demand,
    inflow_reach,
    w_in,
    w_hid,
    w_out,
    block_inverse,
    upstream_coupling,
    discharge_cotangent,
):
    hours, cells = precip.shape
    regions, owners = lax.axis_size("region"), lax.axis_size("cells")
    attrs, hid = w_in.shape
    params = w_out.shape[1]
    reach_count = block_inverse.shape[1]
    lateral_scale = reach_count / cells
    assert 4 * cells == LANES * owners and w_hid.shape[0] == 2
    assert regions & (regions - 1) == 0 and owners & (owners - 1) == 0
    shape = jax.ShapeDtypeStruct

    def in_hbm(array):
        return pltpu.with_memory_space_constraint(array, pltpu.HBM)

    packed, ct, inverse, coupling, inflow, w_in_v, w_hid_v, w_out_v = pl.pallas_call(
        open_kernel,
        out_shape=(
            pltpu.VMEM((owners, hours, LANES), BF16),
            shape((hours, reach_count), F32),
            shape(block_inverse.shape, F32),
            shape(upstream_coupling.shape, F32),
            shape((1, cells), jnp.int32),
            shape(w_in.shape, BF16),
            shape(w_hid.shape, BF16),
            shape((16, hid), BF16),
        ),
        in_specs=[HBM] * 10,
        out_specs=(VMEM,) * 8,
        scratch_shapes=[
            pltpu.VMEM((attrs, cells), BF16),
            pltpu.VMEM((hours, cells), BF16),
            pltpu.VMEM((hours, cells), BF16),
            pltpu.VMEM((params, hid), BF16),
            pltpu.SemaphoreType.DMA((10,)),
        ],
        compiler_params=pltpu.CompilerParams(vmem_limit_bytes=8 << 20),
        name="open",
    )(
        in_hbm(attributes),
        in_hbm(precip),
        in_hbm(pet_demand),
        in_hbm(discharge_cotangent),
        in_hbm(block_inverse),
        in_hbm(upstream_coupling),
        in_hbm(inflow_reach.reshape(1, cells)),
        in_hbm(w_in),
        in_hbm(w_hid),
        in_hbm(w_out.T),
    )
    arrived = lax.all_to_all(
        packed,
        "cells",
        split_axis=0,
        concat_axis=0,
        tiled=True,
        axis_index_groups=[[place(k, owners) for k in range(owners)]],
    )

    start_ct = dot_high(ct, inverse, NT)
    outgoing = dot_high(start_ct, coupling, NT)
    incoming = jnp.zeros_like(start_ct)
    for step in range(regions - 1):
        if step:
            lateral_ct = start_ct + dot_high(incoming, inverse, NT)
            outgoing = dot_high(lateral_ct, coupling, NT)
        if regions == 2:
            incoming = exchange(outgoing, 1, 0)
        else:
            incoming = shifted(outgoing, "region", -1)

    rows = hid + attrs
    runoff, keep, send = pl.pallas_call(
        functools.partial(main_kernel, lateral_scale),
        out_shape=(
            shape((hours, cells), BF16),
            shape((rows, hid), BF16),
            shape((rows, hid), BF16),
        ),
        in_specs=[VMEM] * 8,
        out_specs=(VMEM, VMEM, VMEM),
        scratch_shapes=[
            pltpu.VMEM((hours, cells), F32),
            pltpu.VMEM((hours, cells), F32),
            pltpu.VMEM((attrs, cells), F32),
            pltpu.VMEM((hours, cells), F32),
            pltpu.VMEM((hours, cells), F32),
        ],
        compiler_params=pltpu.CompilerParams(vmem_limit_bytes=32 << 20),
        name="model",
    )(arrived, start_ct, incoming, inverse, inflow, w_in_v, w_hid_v, w_out_v)

    total = keep.astype(F32) + exchange(send, 0, 1).astype(F32)
    onehot = (inflow[0][:, None] == jnp.arange(reach_count, dtype=jnp.int32)[None, :]).astype(
        BF16
    )
    lateral = dot(runoff, onehot) * lateral_scale
    discharge = dot_high(lateral, inverse)
    bits = [(1 << b, 0) for b in range(regions.bit_length() - 1)]
    bits += [(0, 1 << b) for b in range(1, owners.bit_length() - 1)]
    stages = [bits[k : k + 2] for k in range(0, len(bits), 2)]
    if regions != 2:
        for _ in range(regions - 1):
            incoming = shifted(discharge, "region", 1)
            discharge = dot_high(lateral + dot_high(incoming, coupling), inverse)
    for stage, pair in enumerate(stages):
        block = lax.optimization_barrier(total.astype(BF16))
        bundle = block
        if stage == 0 and regions == 2:
            upper = lax.reduce_precision(discharge, 8, 7)
            bundle = jnp.concatenate(
                [block, upper.astype(BF16), (discharge - upper).astype(BF16)], axis=0
            )
        first = exchange(bundle, *pair[0])
        parts = [block, first[:rows]]
        if len(pair) == 2:
            (r0, c0), (r1, c1) = pair
            parts += [exchange(block, r1, c1), exchange(block, r0 ^ r1, c0 ^ c1)]
        parts = [p.astype(F32) for p in parts]
        total = parts[0] + parts[1]
        if len(pair) == 2:
            total = total + (parts[2] + parts[3])
        if stage == 0 and regions == 2:
            upper, lower = first[rows : rows + hours], first[rows + hours :]
            incoming = upper.astype(F32) + lower.astype(F32)
            incoming = jnp.where(lax.axis_index("region") == 0, 0.0, incoming)
            discharge = dot_high(lateral + dot_high(incoming, coupling), inverse)
    other = exchange(total, 0, 1)

    grad_in, grad_hid, grad_out = pl.pallas_call(
        functools.partial(finish_kernel, 1.0 / (regions * owners)),
        out_shape=(
            shape((attrs, hid), F32),
            shape((2, hid, hid), F32),
            shape((params, hid), F32),
        ),
        in_specs=[VMEM, VMEM],
        out_specs=(VMEM, VMEM, VMEM),
        compiler_params=pltpu.CompilerParams(vmem_limit_bytes=4 << 20),
        name="finish",
    )(total, other)
    return discharge, grad_in, grad_hid, grad_out.T


def solution(mesh):
    split = ("region", "cells")
    placed = (
        P(None, split),
        P(None, split),
        P(None, split),
        P(split),
        P(),
        P(),
        P(),
        P(split, None),
        P(split, None),
        P(None, split),
    )
    return jax.shard_map(
        per_device,
        mesh=mesh,
        in_specs=placed,
        out_specs=(P(None, split), P(), P(), P()),
        check_vma=False,
    )
```

```python
import functools

import jax
import jax.numpy as jnp
from jax import lax
from jax.experimental import pallas as pl
from jax.experimental.pallas import tpu as pltpu
from jax.sharding import PartitionSpec as P

F32 = jnp.float32
BF16 = jnp.bfloat16
LANES = 128
VMEM = pl.BlockSpec(memory_space=pltpu.VMEM)
HBM = pl.BlockSpec(memory_space=pltpu.HBM)
NT = (((1,), (1,)), ((), ()))
TN = (((0,), (0,)), ((), ()))


def dot(left, right, dims=(((1,), (0,)), ((), ()))):
    return lax.dot_general(left, right, dims, preferred_element_type=F32)


def dot_high(left, right, dims=(((1,), (0,)), ((), ()))):
    return lax.dot_general(
        left, right, dims, precision=lax.Precision.HIGHEST, preferred_element_type=F32
    )


def shifted(block, axis, distance):
    devices = range(lax.axis_size(axis))
    route = [(i - distance, i) for i in devices if i - distance in devices]
    return lax.ppermute(block, axis, route)


def place(device, devices):
    return device ^ (devices // 2 + 3)


def swap_groups(group):
    lane = lax.broadcasted_iota(jnp.int32, group[0].shape, 1)
    half, quarter = LANES // 2, LANES // 4
    low = lane < half
    wide = [None] * 4
    for k in range(2):
        wide[k] = jnp.where(low, group[k], pltpu.roll(group[k + 2], half, 1))
        wide[k + 2] = jnp.where(low, pltpu.roll(group[k], half, 1), group[k + 2])
    even = lane % half < quarter
    out = [None] * 4
    for k in (0, 2):
        out[k] = jnp.where(even, wide[k], pltpu.roll(wide[k + 1], quarter, 1))
        out[k + 1] = jnp.where(even, pltpu.roll(wide[k], LANES - quarter, 1), wide[k + 1])
    return out


def open_kernel(
    attr_hbm,
    rain_ref,
    demand_ref,
    ct_hbm,
    inverse_hbm,
    coupling_hbm,
    inflow_hbm,
    w_in_hbm,
    w_hid_hbm,
    w_out_rows_ref,
    packed_ref,
    ct_ref,
    inverse_ref,
    coupling_ref,
    inflow_ref,
    w_in_ref,
    w_hid_ref,
    w_out_ref,
    attr_s,
    sems,
):
    pairs = [
        (attr_hbm, attr_s),
        (ct_hbm, ct_ref),
        (inverse_hbm, inverse_ref),
        (coupling_hbm, coupling_ref),
        (w_hid_hbm, w_hid_ref),
        (w_in_hbm, w_in_ref),
        (inflow_hbm, inflow_ref),
    ]
    copies = [pltpu.make_async_copy(a, b, sems.at[i]) for i, (a, b) in enumerate(pairs)]
    for copy in copies:
        copy.start()
    hours, cells = rain_ref.shape
    half = attr_s.shape[0] // 2
    copies[0].wait()
    attr = attr_s[...].astype(F32)
    fill = jnp.zeros((hours - half, cells), F32)
    rows = [
        rain_ref[...].astype(F32),
        demand_ref[...].astype(F32),
        jnp.concatenate([attr[:half], fill], axis=0),
        jnp.concatenate([attr[half:], fill], axis=0),
    ]
    for column in range(cells // LANES):
        window = slice(column * LANES, (column + 1) * LANES)
        for k, block in enumerate(swap_groups([r[:, window] for r in rows])):
            packed_ref[place(4 * column + k, packed_ref.shape[0])] = block.astype(BF16)
    for copy in copies[1:]:
        copy.wait()
    out = w_out_rows_ref[...].astype(F32)
    wide = jnp.zeros((w_out_ref.shape[0] - out.shape[0], out.shape[1]), F32)
    w_out_ref[...] = jnp.concatenate([out, wide], axis=0).astype(BF16)


def received_cotangent(scale, start_ref, incoming_ref, inverse_ref, inflow_ref):
    last = lax.axis_index("region") == lax.axis_size("region") - 1
    incoming = jnp.where(last, 0.0, incoming_ref[...])
    lateral_ct = start_ref[...] + dot_high(incoming, inverse_ref[...], NT)
    scaled = (lateral_ct * scale).astype(BF16)
    shape = (scaled.shape[1], inflow_ref.shape[1])
    onehot = (
        jnp.broadcast_to(inflow_ref[...], shape) == lax.broadcasted_iota(jnp.int32, shape, 0)
    ).astype(F32)
    return dot(scaled, onehot.astype(BF16)).astype(BF16).astype(F32)


def main_kernel(
    scale,
    packed_ref,
    start_ref,
    incoming_ref,
    inverse_ref,
    inflow_ref,
    w_in_ref,
    w_hid_ref,
    w_out_ref,
    runoff_ref,
    keep_ref,
    send_ref,
    rain_s,
    demand_s,
    attr_s,
    x_s,
    carry_s,
):
    hours, cells = rain_s.shape
    half = attr_s.shape[0] // 2
    for column in range(cells // LANES):
        window = slice(column * LANES, (column + 1) * LANES)
        rain, demand, first, second = swap_groups(
            [
                packed_ref[place(4 * column + k, packed_ref.shape[0])].astype(F32)
                for k in range(4)
            ]
        )
        rain_s[:, window] = rain
        demand_s[:, window] = demand
        attr_s[:half, window] = first[:half]
        attr_s[half:, window] = second[:half]

    layers = w_hid_ref.shape[0]
    attr = attr_s[...].astype(BF16)
    wide = [jnp.tanh(dot(w_in_ref[...], attr, TN))]
    hidden = [wide[0].astype(BF16)]
    for layer in range(layers):
        wide.append(jnp.tanh(dot(w_hid_ref[layer], hidden[-1], TN)))
        hidden.append(wide[-1].astype(BF16))
    w_out = w_out_ref[...]
    params = dot(w_out, hidden[-1])[:8]
    gate = jax.nn.sigmoid(params)
    gate0, gate1, gate2, gate3 = (gate[i : i + 1] for i in range(4))
    drain = 0.02 + 0.3 * gate0
    capacity = 1.0 + 4.0 * gate1
    evap = 0.3 * gate2
    storage = gate3 * capacity

    demand = demand_s[...]
    kept = (1.0 - drain) - evap * demand
    carry_s[...] = kept
    rain_s[...] = rain_s[...] - capacity
    for hour in range(hours):
        x = storage + rain_s[hour : hour + 1]
        x_s[hour : hour + 1] = x
        under = jnp.maximum(-x, 0.0) + jnp.log(1.0 + jnp.exp(-jnp.abs(x)))
        storage = (capacity - under) * carry_s[hour : hour + 1]

    x = x_s[...]
    ct = received_cotangent(scale, start_ref, incoming_ref, inverse_ref, inflow_ref)
    small = jnp.exp(-jnp.abs(x))
    log = jnp.log(1.0 + small)
    spill = jnp.maximum(x, 0.0) + log
    level = capacity - (jnp.maximum(-x, 0.0) + log)
    runoff_ref[...] = (spill + drain * level).astype(BF16)
    share = 1.0 / (1.0 + small)
    slope = jnp.where(x >= 0.0, share, small * share)
    rest = 1.0 - slope
    x_s[...] = kept * rest
    rain_s[...] = ct * (drain * rest + slope)
    carry = jnp.zeros((1, cells), F32)
    for hour in range(hours - 1, -1, -1):
        carry_s[hour : hour + 1] = carry
        carry = carry * x_s[hour : hour + 1] + rain_s[hour : hour + 1]
    after = carry_s[...]
    level_ct = after * kept + ct * drain
    capacity_ct = -jnp.sum(slope * (ct - level_ct), axis=0, keepdims=True)
    held = after * level
    drain_ct = jnp.sum(level * ct - held, axis=0, keepdims=True)
    evap_ct = -jnp.sum(held * demand, axis=0, keepdims=True)
    capacity_ct = capacity_ct + carry * gate3
    params_ct = jnp.concatenate(
        [
            drain_ct * (0.3 * gate0 * (1.0 - gate0)),
            capacity_ct * (4.0 * gate1 * (1.0 - gate1)),
            evap_ct * (0.3 * gate2 * (1.0 - gate2)),
            carry * capacity * (gate3 * (1.0 - gate3)),
            jnp.zeros((w_out.shape[0] - 4, cells), F32),
        ],
        axis=0,
    ).astype(BF16)

    grad_out = dot(params_ct, hidden[-1], NT)
    back = dot(w_out, params_ct, TN)
    grads = [None] * layers
    for layer in range(layers - 1, -1, -1):
        top = wide[layer + 1]
        g = (back * (1.0 - top * top)).astype(BF16)
        grads[layer] = dot(hidden[layer], g, NT)
        back = dot(w_hid_ref[layer], g)
    g = (back * (1.0 - wide[0] * wide[0])).astype(BF16)
    grad_in = dot(attr, g, NT)

    rows, width = keep_ref.shape
    fill = rows - grads[1].shape[0] - grad_out.shape[0]
    first = jnp.concatenate([grads[0], grad_in], axis=0)
    second = jnp.concatenate([grads[1], grad_out, jnp.zeros((fill, width), F32)], axis=0)
    lower = lax.axis_index("cells") & 1 == 0

    @pl.when(lower)
    def _():
        keep_ref[...] = first.astype(BF16)
        send_ref[...] = second.astype(BF16)

    @pl.when(jnp.logical_not(lower))
    def _():
        keep_ref[...] = second.astype(BF16)
        send_ref[...] = first.astype(BF16)


def finish_kernel(scale, mine_ref, other_ref, grad_in_ref, grad_hid_ref, grad_out_ref):
    hid = grad_hid_ref.shape[1]
    params = grad_out_ref.shape[0]

    def place(first, second):
        grad_hid_ref[0] = first[:hid] * scale
        grad_in_ref[...] = first[hid:] * scale
        grad_hid_ref[1] = second[:hid] * scale
        grad_out_ref[...] = second[hid : hid + params] * scale

    lower = lax.axis_index("cells") & 1 == 0

    @pl.when(lower)
    def _():
        place(mine_ref, other_ref)

    @pl.when(jnp.logical_not(lower))
    def _():
        place(other_ref, mine_ref)


def exchange(block, region_flip, cells_flip):
    regions, cells = lax.axis_size("region"), lax.axis_size("cells")
    route = [
        (r * cells + c, (r ^ region_flip) * cells + (c ^ cells_flip))
        for r in range(regions)
        for c in range(cells)
    ]
    return lax.ppermute(block, ("region", "cells"), route)


def per_device(
    attributes,
    precip,
    pet_demand,
    inflow_reach,
    w_in,
    w_hid,
    w_out,
    block_inverse,
    upstream_coupling,
    discharge_cotangent,
):
    hours, cells = precip.shape
    regions, owners = lax.axis_size("region"), lax.axis_size("cells")
    attrs, hid = w_in.shape
    params = w_out.shape[1]
    reach_count = block_inverse.shape[1]
    lateral_scale = reach_count / cells
    assert 4 * cells == LANES * owners and w_hid.shape[0] == 2
    assert regions & (regions - 1) == 0 and owners & (owners - 1) == 0
    shape = jax.ShapeDtypeStruct

    def in_hbm(array):
        return pltpu.with_memory_space_constraint(array, pltpu.HBM)

    packed, ct, inverse, coupling, inflow, w_in_v, w_hid_v, w_out_v = pl.pallas_call(
        open_kernel,
        out_shape=(
            pltpu.VMEM((owners, hours, LANES), BF16),
            shape((hours, reach_count), F32),
            shape(block_inverse.shape, F32),
            shape(upstream_coupling.shape, F32),
            shape((1, cells), jnp.int32),
            shape(w_in.shape, BF16),
            shape(w_hid.shape, BF16),
            shape((16, hid), BF16),
        ),
        in_specs=[HBM, VMEM, VMEM] + [HBM] * 6 + [VMEM],
        out_specs=(VMEM,) * 8,
        scratch_shapes=[
            pltpu.VMEM((attrs, cells), BF16),
            pltpu.SemaphoreType.DMA((7,)),
        ],
        compiler_params=pltpu.CompilerParams(vmem_limit_bytes=8 << 20),
        name="open",
    )(
        in_hbm(attributes),
        in_hbm(precip),
        in_hbm(pet_demand),
        in_hbm(discharge_cotangent),
        in_hbm(block_inverse),
        in_hbm(upstream_coupling),
        in_hbm(inflow_reach.reshape(1, cells)),
        in_hbm(w_in),
        in_hbm(w_hid),
        in_hbm(w_out.T),
    )
    arrived = lax.all_to_all(
        packed,
        "cells",
        split_axis=0,
        concat_axis=0,
        tiled=True,
        axis_index_groups=[[place(k, owners) for k in range(owners)]],
    )

    start_ct = dot_high(ct, inverse, NT)
    outgoing = dot_high(start_ct, coupling, NT)
    incoming = jnp.zeros_like(start_ct)
    for step in range(regions - 1):
        if step:
            lateral_ct = start_ct + dot_high(incoming, inverse, NT)
            outgoing = dot_high(lateral_ct, coupling, NT)
        if regions == 2:
            incoming = exchange(outgoing, 1, 0)
        else:
            incoming = shifted(outgoing, "region", -1)

    rows = hid + attrs
    runoff, keep, send = pl.pallas_call(
        functools.partial(main_kernel, lateral_scale),
        out_shape=(
            shape((hours, cells), BF16),
            shape((rows, hid), BF16),
            shape((rows, hid), BF16),
        ),
        in_specs=[VMEM] * 8,
        out_specs=(VMEM, VMEM, VMEM),
        scratch_shapes=[
            pltpu.VMEM((hours, cells), F32),
            pltpu.VMEM((hours, cells), F32),
            pltpu.VMEM((attrs, cells), F32),
            pltpu.VMEM((hours, cells), F32),
            pltpu.VMEM((hours, cells), F32),
        ],
        compiler_params=pltpu.CompilerParams(vmem_limit_bytes=32 << 20),
        name="model",
    )(arrived, start_ct, incoming, inverse, inflow, w_in_v, w_hid_v, w_out_v)

    total = keep.astype(F32) + exchange(send, 0, 1).astype(F32)
    onehot = (inflow[0][:, None] == jnp.arange(reach_count, dtype=jnp.int32)[None, :]).astype(
        BF16
    )
    lateral = dot(runoff, onehot) * lateral_scale
    discharge = dot_high(lateral, inverse)
    bits = [(1 << b, 0) for b in range(regions.bit_length() - 1)]
    bits += [(0, 1 << b) for b in range(1, owners.bit_length() - 1)]
    stages = [bits[k : k + 2] for k in range(0, len(bits), 2)]
    if regions != 2:
        for _ in range(regions - 1):
            incoming = shifted(discharge, "region", 1)
            discharge = dot_high(lateral + dot_high(incoming, coupling), inverse)
    for stage, pair in enumerate(stages):
        block = lax.optimization_barrier(total.astype(BF16))
        bundle = block
        if stage == 0 and regions == 2:
            upper = lax.reduce_precision(discharge, 8, 7)
            bundle = jnp.concatenate(
                [block, upper.astype(BF16), (discharge - upper).astype(BF16)], axis=0
            )
        first = exchange(bundle, *pair[0])
        parts = [block, first[:rows]]
        if len(pair) == 2:
            (r0, c0), (r1, c1) = pair
            parts += [exchange(block, r1, c1), exchange(block, r0 ^ r1, c0 ^ c1)]
        parts = [p.astype(F32) for p in parts]
        total = parts[0] + parts[1]
        if len(pair) == 2:
            total = total + (parts[2] + parts[3])
        if stage == 0 and regions == 2:
            upper, lower = first[rows : rows + hours], first[rows + hours :]
            incoming = upper.astype(F32) + lower.astype(F32)
            incoming = jnp.where(lax.axis_index("region") == 0, 0.0, incoming)
            discharge = dot_high(lateral + dot_high(incoming, coupling), inverse)
    other = exchange(total, 0, 1)

    grad_in, grad_hid, grad_out = pl.pallas_call(
        functools.partial(finish_kernel, 1.0 / (regions * owners)),
        out_shape=(
            shape((attrs, hid), F32),
            shape((2, hid, hid), F32),
            shape((params, hid), F32),
        ),
        in_specs=[VMEM, VMEM],
        out_specs=(VMEM, VMEM, VMEM),
        compiler_params=pltpu.CompilerParams(vmem_limit_bytes=4 << 20),
        name="finish",
    )(total, other)
    return discharge, grad_in, grad_hid, grad_out.T


def solution(mesh):
    split = ("region", "cells")
    placed = (
        P(None, split),
        P(None, split),
        P(None, split),
        P(split),
        P(),
        P(),
        P(),
        P(split, None),
        P(split, None),
        P(None, split),
    )
    return jax.shard_map(
        per_device,
        mesh=mesh,
        in_specs=placed,
        out_specs=(P(None, split), P(), P(), P()),
        check_vma=False,
    )
```

```python
import functools

import jax
import jax.numpy as jnp
from jax import lax
from jax.experimental import pallas as pl
from jax.experimental.pallas import tpu as pltpu
from jax.sharding import PartitionSpec as P

F32 = jnp.float32
BF16 = jnp.bfloat16
LANES = 128
VMEM = pl.BlockSpec(memory_space=pltpu.VMEM)
NT = (((1,), (1,)), ((), ()))
TN = (((0,), (0,)), ((), ()))


def dot(left, right, dims=(((1,), (0,)), ((), ()))):
    return lax.dot_general(left, right, dims, preferred_element_type=F32)


def dot_high(left, right, dims=(((1,), (0,)), ((), ()))):
    return lax.dot_general(
        left, right, dims, precision=lax.Precision.HIGHEST, preferred_element_type=F32
    )


def shifted(block, axis, distance):
    devices = range(lax.axis_size(axis))
    route = [(i - distance, i) for i in devices if i - distance in devices]
    return lax.ppermute(block, axis, route)


def place(device, devices):
    return device ^ (devices // 2 + 3)


def swap_groups(group):
    lane = lax.broadcasted_iota(jnp.int32, group[0].shape, 1)
    half, quarter = LANES // 2, LANES // 4
    low = lane < half
    wide = [None] * 4
    for k in range(2):
        wide[k] = jnp.where(low, group[k], pltpu.roll(group[k + 2], half, 1))
        wide[k + 2] = jnp.where(low, pltpu.roll(group[k], half, 1), group[k + 2])
    even = lane % half < quarter
    out = [None] * 4
    for k in (0, 2):
        out[k] = jnp.where(even, wide[k], pltpu.roll(wide[k + 1], quarter, 1))
        out[k + 1] = jnp.where(even, pltpu.roll(wide[k], LANES - quarter, 1), wide[k + 1])
    return out


def open_kernel(
    attr_in,
    rain_in,
    demand_in,
    ct_in,
    inverse_in,
    coupling_in,
    inflow_in,
    w_in_in,
    w_hid_in,
    w_out_in,
    packed_ref,
    ct_ref,
    inverse_ref,
    coupling_ref,
    inflow_ref,
    w_in_ref,
    w_hid_ref,
    w_out_ref,
):
    hours, cells = rain_in.shape
    half = attr_in.shape[0] // 2
    attr = attr_in[...].astype(F32)
    fill = jnp.zeros((hours - half, cells), F32)
    rows = [
        rain_in[...].astype(F32),
        demand_in[...].astype(F32),
        jnp.concatenate([attr[:half], fill], axis=0),
        jnp.concatenate([attr[half:], fill], axis=0),
    ]
    for column in range(cells // LANES):
        window = slice(column * LANES, (column + 1) * LANES)
        for k, block in enumerate(swap_groups([r[:, window] for r in rows])):
            packed_ref[place(4 * column + k, packed_ref.shape[0])] = block.astype(BF16)
    ct_ref[...] = ct_in[...]
    inverse_ref[...] = inverse_in[...]
    coupling_ref[...] = coupling_in[...]
    inflow_ref[...] = inflow_in[...]
    w_in_ref[...] = w_in_in[...]
    w_hid_ref[...] = w_hid_in[...]
    out = w_out_in[...].astype(F32)
    wide = jnp.zeros((w_out_ref.shape[0] - out.shape[0], out.shape[1]), F32)
    w_out_ref[...] = jnp.concatenate([out, wide], axis=0).astype(BF16)


def received_cotangent(scale, start_ref, incoming_ref, inverse_ref, inflow_ref):
    last = lax.axis_index("region") == lax.axis_size("region") - 1
    incoming = jnp.where(last, 0.0, incoming_ref[...])
    lateral_ct = start_ref[...] + dot_high(incoming, inverse_ref[...], NT)
    scaled = (lateral_ct * scale).astype(BF16)
    shape = (scaled.shape[1], inflow_ref.shape[1])
    onehot = (
        jnp.broadcast_to(inflow_ref[...], shape) == lax.broadcasted_iota(jnp.int32, shape, 0)
    ).astype(F32)
    return dot(scaled, onehot.astype(BF16)).astype(BF16).astype(F32)


def main_kernel(
    scale,
    packed_ref,
    start_ref,
    incoming_ref,
    inverse_ref,
    inflow_ref,
    w_in_ref,
    w_hid_ref,
    w_out_ref,
    runoff_ref,
    keep_ref,
    send_ref,
    rain_s,
    demand_s,
    attr_s,
    x_s,
    carry_s,
):
    hours, cells = rain_s.shape
    half = attr_s.shape[0] // 2
    for column in range(cells // LANES):
        window = slice(column * LANES, (column + 1) * LANES)
        rain, demand, first, second = swap_groups(
            [
                packed_ref[place(4 * column + k, packed_ref.shape[0])].astype(F32)
                for k in range(4)
            ]
        )
        rain_s[:, window] = rain
        demand_s[:, window] = demand
        attr_s[:half, window] = first[:half]
        attr_s[half:, window] = second[:half]

    layers = w_hid_ref.shape[0]
    attr = attr_s[...].astype(BF16)
    wide = [jnp.tanh(dot(w_in_ref[...], attr, TN))]
    hidden = [wide[0].astype(BF16)]
    for layer in range(layers):
        wide.append(jnp.tanh(dot(w_hid_ref[layer], hidden[-1], TN)))
        hidden.append(wide[-1].astype(BF16))
    w_out = w_out_ref[...]
    params = dot(w_out, hidden[-1])[:8]
    gate = jax.nn.sigmoid(params)
    gate0, gate1, gate2, gate3 = (gate[i : i + 1] for i in range(4))
    drain = 0.02 + 0.3 * gate0
    capacity = 1.0 + 4.0 * gate1
    evap = 0.3 * gate2
    storage = gate3 * capacity

    demand = demand_s[...]
    kept = (1.0 - drain) - evap * demand
    carry_s[...] = kept
    rain_s[...] = rain_s[...] - capacity
    for hour in range(hours):
        x = storage + rain_s[hour : hour + 1]
        x_s[hour : hour + 1] = x
        under = jnp.maximum(-x, 0.0) + jnp.log(1.0 + jnp.exp(-jnp.abs(x)))
        storage = (capacity - under) * carry_s[hour : hour + 1]

    x = x_s[...]
    ct = received_cotangent(scale, start_ref, incoming_ref, inverse_ref, inflow_ref)
    small = jnp.exp(-jnp.abs(x))
    log = jnp.log(1.0 + small)
    spill = jnp.maximum(x, 0.0) + log
    level = capacity - (jnp.maximum(-x, 0.0) + log)
    runoff_ref[...] = (spill + drain * level).astype(BF16)
    share = 1.0 / (1.0 + small)
    slope = jnp.where(x >= 0.0, share, small * share)
    rest = 1.0 - slope
    x_s[...] = kept * rest
    rain_s[...] = ct * (drain * rest + slope)
    carry = jnp.zeros((1, cells), F32)
    for hour in range(hours - 1, -1, -1):
        carry_s[hour : hour + 1] = carry
        carry = carry * x_s[hour : hour + 1] + rain_s[hour : hour + 1]
    after = carry_s[...]
    level_ct = after * kept + ct * drain
    capacity_ct = -jnp.sum(slope * (ct - level_ct), axis=0, keepdims=True)
    held = after * level
    drain_ct = jnp.sum(level * ct - held, axis=0, keepdims=True)
    evap_ct = -jnp.sum(held * demand, axis=0, keepdims=True)
    capacity_ct = capacity_ct + carry * gate3
    params_ct = jnp.concatenate(
        [
            drain_ct * (0.3 * gate0 * (1.0 - gate0)),
            capacity_ct * (4.0 * gate1 * (1.0 - gate1)),
            evap_ct * (0.3 * gate2 * (1.0 - gate2)),
            carry * capacity * (gate3 * (1.0 - gate3)),
            jnp.zeros((w_out.shape[0] - 4, cells), F32),
        ],
        axis=0,
    ).astype(BF16)

    grad_out = dot(params_ct, hidden[-1], NT)
    back = dot(w_out, params_ct, TN)
    grads = [None] * layers
    for layer in range(layers - 1, -1, -1):
        top = wide[layer + 1]
        g = (back * (1.0 - top * top)).astype(BF16)
        grads[layer] = dot(hidden[layer], g, NT)
        back = dot(w_hid_ref[layer], g)
    g = (back * (1.0 - wide[0] * wide[0])).astype(BF16)
    grad_in = dot(attr, g, NT)

    rows, width = keep_ref.shape
    fill = rows - grads[1].shape[0] - grad_out.shape[0]
    first = jnp.concatenate([grads[0], grad_in], axis=0)
    second = jnp.concatenate([grads[1], grad_out, jnp.zeros((fill, width), F32)], axis=0)
    lower = lax.axis_index("cells") & 1 == 0

    @pl.when(lower)
    def _():
        keep_ref[...] = first.astype(BF16)
        send_ref[...] = second.astype(BF16)

    @pl.when(jnp.logical_not(lower))
    def _():
        keep_ref[...] = second.astype(BF16)
        send_ref[...] = first.astype(BF16)


def finish_kernel(scale, mine_ref, other_ref, grad_in_ref, grad_hid_ref, grad_out_ref):
    hid = grad_hid_ref.shape[1]
    params = grad_out_ref.shape[0]

    def place(first, second):
        grad_hid_ref[0] = first[:hid] * scale
        grad_in_ref[...] = first[hid:] * scale
        grad_hid_ref[1] = second[:hid] * scale
        grad_out_ref[...] = second[hid : hid + params] * scale

    lower = lax.axis_index("cells") & 1 == 0

    @pl.when(lower)
    def _():
        place(mine_ref, other_ref)

    @pl.when(jnp.logical_not(lower))
    def _():
        place(other_ref, mine_ref)


def exchange(block, region_flip, cells_flip):
    regions, cells = lax.axis_size("region"), lax.axis_size("cells")
    route = [
        (r * cells + c, (r ^ region_flip) * cells + (c ^ cells_flip))
        for r in range(regions)
        for c in range(cells)
    ]
    return lax.ppermute(block, ("region", "cells"), route)


def per_device(
    attributes,
    precip,
    pet_demand,
    inflow_reach,
    w_in,
    w_hid,
    w_out,
    block_inverse,
    upstream_coupling,
    discharge_cotangent,
):
    hours, cells = precip.shape
    regions, owners = lax.axis_size("region"), lax.axis_size("cells")
    attrs, hid = w_in.shape
    params = w_out.shape[1]
    reach_count = block_inverse.shape[1]
    lateral_scale = reach_count / cells
    assert 4 * cells == LANES * owners and w_hid.shape[0] == 2
    assert regions & (regions - 1) == 0 and owners & (owners - 1) == 0
    shape = jax.ShapeDtypeStruct

    def in_hbm(array):
        return pltpu.with_memory_space_constraint(array, pltpu.HBM)

    packed, ct, inverse, coupling, inflow, w_in_v, w_hid_v, w_out_v = pl.pallas_call(
        open_kernel,
        out_shape=(
            pltpu.VMEM((owners, hours, LANES), BF16),
            shape((hours, reach_count), F32),
            shape(block_inverse.shape, F32),
            shape(upstream_coupling.shape, F32),
            shape((1, cells), jnp.int32),
            shape(w_in.shape, BF16),
            shape(w_hid.shape, BF16),
            shape((16, hid), BF16),
        ),
        in_specs=[VMEM] * 10,
        out_specs=(VMEM,) * 8,
        compiler_params=pltpu.CompilerParams(vmem_limit_bytes=8 << 20),
        name="open",
    )(
        in_hbm(attributes),
        in_hbm(precip),
        in_hbm(pet_demand),
        in_hbm(discharge_cotangent),
        in_hbm(block_inverse),
        in_hbm(upstream_coupling),
        in_hbm(inflow_reach.reshape(1, cells)),
        in_hbm(w_in),
        in_hbm(w_hid),
        in_hbm(w_out.T),
    )
    arrived = lax.all_to_all(
        packed,
        "cells",
        split_axis=0,
        concat_axis=0,
        tiled=True,
        axis_index_groups=[[place(k, owners) for k in range(owners)]],
    )

    start_ct = dot_high(ct, inverse, NT)
    outgoing = dot_high(start_ct, coupling, NT)
    incoming = jnp.zeros_like(start_ct)
    for step in range(regions - 1):
        if step:
            lateral_ct = start_ct + dot_high(incoming, inverse, NT)
            outgoing = dot_high(lateral_ct, coupling, NT)
        if regions == 2:
            incoming = exchange(outgoing, 1, 0)
        else:
            incoming = shifted(outgoing, "region", -1)

    rows = hid + attrs
    runoff, keep, send = pl.pallas_call(
        functools.partial(main_kernel, lateral_scale),
        out_shape=(
            shape((hours, cells), BF16),
            shape((rows, hid), BF16),
            shape((rows, hid), BF16),
        ),
        in_specs=[VMEM] * 8,
        out_specs=(VMEM, VMEM, VMEM),
        scratch_shapes=[
            pltpu.VMEM((hours, cells), F32),
            pltpu.VMEM((hours, cells), F32),
            pltpu.VMEM((attrs, cells), F32),
            pltpu.VMEM((hours, cells), F32),
            pltpu.VMEM((hours, cells), F32),
        ],
        compiler_params=pltpu.CompilerParams(vmem_limit_bytes=32 << 20),
        name="model",
    )(arrived, start_ct, incoming, inverse, inflow, w_in_v, w_hid_v, w_out_v)

    total = keep.astype(F32) + exchange(send, 0, 1).astype(F32)
    onehot = (inflow[0][:, None] == jnp.arange(reach_count, dtype=jnp.int32)[None, :]).astype(
        BF16
    )
    lateral = dot(runoff, onehot) * lateral_scale
    discharge = dot_high(lateral, inverse)
    bits = [(1 << b, 0) for b in range(regions.bit_length() - 1)]
    bits += [(0, 1 << b) for b in range(1, owners.bit_length() - 1)]
    stages = [bits[k : k + 2] for k in range(0, len(bits), 2)]
    if regions != 2:
        for _ in range(regions - 1):
            incoming = shifted(discharge, "region", 1)
            discharge = dot_high(lateral + dot_high(incoming, coupling), inverse)
    for stage, pair in enumerate(stages):
        block = lax.optimization_barrier(total.astype(BF16))
        bundle = block
        if stage == 0 and regions == 2:
            upper = lax.reduce_precision(discharge, 8, 7)
            bundle = jnp.concatenate(
                [block, upper.astype(BF16), (discharge - upper).astype(BF16)], axis=0
            )
        first = exchange(bundle, *pair[0])
        parts = [block, first[:rows]]
        if len(pair) == 2:
            (r0, c0), (r1, c1) = pair
            parts += [exchange(block, r1, c1), exchange(block, r0 ^ r1, c0 ^ c1)]
        parts = [p.astype(F32) for p in parts]
        total = parts[0] + parts[1]
        if len(pair) == 2:
            total = total + (parts[2] + parts[3])
        if stage == 0 and regions == 2:
            upper, lower = first[rows : rows + hours], first[rows + hours :]
            incoming = upper.astype(F32) + lower.astype(F32)
            incoming = jnp.where(lax.axis_index("region") == 0, 0.0, incoming)
            discharge = dot_high(lateral + dot_high(incoming, coupling), inverse)
    other = exchange(total, 0, 1)

    grad_in, grad_hid, grad_out = pl.pallas_call(
        functools.partial(finish_kernel, 1.0 / (regions * owners)),
        out_shape=(
            shape((attrs, hid), F32),
            shape((2, hid, hid), F32),
            shape((params, hid), F32),
        ),
        in_specs=[VMEM, VMEM],
        out_specs=(VMEM, VMEM, VMEM),
        compiler_params=pltpu.CompilerParams(vmem_limit_bytes=4 << 20),
        name="finish",
    )(total, other)
    return discharge, grad_in, grad_hid, grad_out.T


def solution(mesh):
    split = ("region", "cells")
    placed = (
        P(None, split),
        P(None, split),
        P(None, split),
        P(split),
        P(),
        P(),
        P(),
        P(split, None),
        P(split, None),
        P(None, split),
    )
    return jax.shard_map(
        per_device,
        mesh=mesh,
        in_specs=placed,
        out_specs=(P(None, split), P(), P(), P()),
        check_vma=False,
    )
```

```python
import functools

import jax
import jax.numpy as jnp
from jax import lax
from jax.experimental import pallas as pl
from jax.experimental.pallas import tpu as pltpu
from jax.sharding import PartitionSpec as P

F32 = jnp.float32
BF16 = jnp.bfloat16
LANES = 128
VMEM = pl.BlockSpec(memory_space=pltpu.VMEM)
NT = (((1,), (1,)), ((), ()))
TN = (((0,), (0,)), ((), ()))


def dot(left, right, dims=(((1,), (0,)), ((), ()))):
    return lax.dot_general(left, right, dims, preferred_element_type=F32)


def dot_high(left, right, dims=(((1,), (0,)), ((), ()))):
    return lax.dot_general(
        left, right, dims, precision=lax.Precision.HIGHEST, preferred_element_type=F32
    )


def shifted(block, axis, distance):
    devices = range(lax.axis_size(axis))
    route = [(i - distance, i) for i in devices if i - distance in devices]
    return lax.ppermute(block, axis, route)


def place(device, devices):
    return device ^ (devices // 2 + 3)


def swap_groups(group):
    lane = lax.broadcasted_iota(jnp.int32, group[0].shape, 1)
    half, quarter = LANES // 2, LANES // 4
    low = lane < half
    wide = [None] * 4
    for k in range(2):
        wide[k] = jnp.where(low, group[k], pltpu.roll(group[k + 2], half, 1))
        wide[k + 2] = jnp.where(low, pltpu.roll(group[k], half, 1), group[k + 2])
    even = lane % half < quarter
    out = [None] * 4
    for k in (0, 2):
        out[k] = jnp.where(even, wide[k], pltpu.roll(wide[k + 1], quarter, 1))
        out[k + 1] = jnp.where(even, pltpu.roll(wide[k], LANES - quarter, 1), wide[k + 1])
    return out


def open_kernel(
    attr_in,
    rain_in,
    demand_in,
    ct_in,
    inverse_in,
    coupling_in,
    inflow_in,
    w_in_in,
    w_hid_in,
    w_out_in,
    packed_ref,
    ct_ref,
    inverse_ref,
    coupling_ref,
    inflow_ref,
    w_in_ref,
    w_hid_ref,
    w_out_ref,
):
    hours, cells = rain_in.shape
    half = attr_in.shape[0] // 2
    attr = attr_in[...].astype(F32)
    fill = jnp.zeros((hours - half, cells), F32)
    rows = [
        rain_in[...].astype(F32),
        demand_in[...].astype(F32),
        jnp.concatenate([attr[:half], fill], axis=0),
        jnp.concatenate([attr[half:], fill], axis=0),
    ]
    for column in range(cells // LANES):
        window = slice(column * LANES, (column + 1) * LANES)
        for k, block in enumerate(swap_groups([r[:, window] for r in rows])):
            packed_ref[place(4 * column + k, packed_ref.shape[0])] = block.astype(BF16)
    ct_ref[...] = ct_in[...]
    inverse_ref[...] = inverse_in[...]
    coupling_ref[...] = coupling_in[...]
    inflow_ref[...] = inflow_in[...]
    w_in_ref[...] = w_in_in[...]
    w_hid_ref[...] = w_hid_in[...]
    out = w_out_in[...].astype(F32)
    wide = jnp.zeros((w_out_ref.shape[0] - out.shape[0], out.shape[1]), F32)
    w_out_ref[...] = jnp.concatenate([out, wide], axis=0).astype(BF16)


def received_cotangent(scale, start_ref, incoming_ref, inverse_ref, inflow_ref):
    last = lax.axis_index("region") == lax.axis_size("region") - 1
    incoming = jnp.where(last, 0.0, incoming_ref[...])
    lateral_ct = start_ref[...] + dot_high(incoming, inverse_ref[...], NT)
    scaled = (lateral_ct * scale).astype(BF16)
    shape = (scaled.shape[1], inflow_ref.shape[1])
    onehot = (
        jnp.broadcast_to(inflow_ref[...], shape) == lax.broadcasted_iota(jnp.int32, shape, 0)
    ).astype(F32)
    return dot(scaled, onehot.astype(BF16)).astype(BF16).astype(F32)


def main_kernel(
    scale,
    packed_ref,
    start_ref,
    incoming_ref,
    inverse_ref,
    inflow_ref,
    w_in_ref,
    w_hid_ref,
    w_out_ref,
    runoff_ref,
    keep_ref,
    send_ref,
    rain_s,
    demand_s,
    attr_s,
    x_s,
    carry_s,
):
    hours, cells = rain_s.shape
    half = attr_s.shape[0] // 2
    for column in range(cells // LANES):
        window = slice(column * LANES, (column + 1) * LANES)
        rain, demand, first, second = swap_groups(
            [
                packed_ref[place(4 * column + k, packed_ref.shape[0])].astype(F32)
                for k in range(4)
            ]
        )
        rain_s[:, window] = rain
        demand_s[:, window] = demand
        attr_s[:half, window] = first[:half]
        attr_s[half:, window] = second[:half]

    layers = w_hid_ref.shape[0]
    attr = attr_s[...].astype(BF16)
    wide = [jnp.tanh(dot(w_in_ref[...], attr, TN))]
    hidden = [wide[0].astype(BF16)]
    for layer in range(layers):
        wide.append(jnp.tanh(dot(w_hid_ref[layer], hidden[-1], TN)))
        hidden.append(wide[-1].astype(BF16))
    w_out = w_out_ref[...]
    params = dot(w_out, hidden[-1])[:8]
    gate = jax.nn.sigmoid(params)
    gate0, gate1, gate2, gate3 = (gate[i : i + 1] for i in range(4))
    drain = 0.02 + 0.3 * gate0
    capacity = 1.0 + 4.0 * gate1
    evap = 0.3 * gate2
    storage = gate3 * capacity

    demand = demand_s[...]
    kept = (1.0 - drain) - evap * demand
    carry_s[...] = kept
    rain_s[...] = rain_s[...] - capacity
    for hour in range(hours):
        x = storage + rain_s[hour : hour + 1]
        x_s[hour : hour + 1] = x
        under = jnp.maximum(-x, 0.0) + jnp.log(1.0 + jnp.exp(-jnp.abs(x)))
        storage = (capacity - under) * carry_s[hour : hour + 1]

    x = x_s[...]
    ct = received_cotangent(scale, start_ref, incoming_ref, inverse_ref, inflow_ref)
    small = jnp.exp(-jnp.abs(x))
    log = jnp.log(1.0 + small)
    spill = jnp.maximum(x, 0.0) + log
    level = capacity - (jnp.maximum(-x, 0.0) + log)
    runoff_ref[...] = (spill + drain * level).astype(BF16)
    share = 1.0 / (1.0 + small)
    slope = jnp.where(x >= 0.0, share, small * share)
    rest = 1.0 - slope
    x_s[...] = kept * rest
    rain_s[...] = ct * (drain * rest + slope)
    carry = jnp.zeros((1, cells), F32)
    for hour in range(hours - 1, -1, -1):
        carry_s[hour : hour + 1] = carry
        carry = carry * x_s[hour : hour + 1] + rain_s[hour : hour + 1]
    after = carry_s[...]
    level_ct = after * kept + ct * drain
    capacity_ct = -jnp.sum(slope * (ct - level_ct), axis=0, keepdims=True)
    held = after * level
    drain_ct = jnp.sum(level * ct - held, axis=0, keepdims=True)
    evap_ct = -jnp.sum(held * demand, axis=0, keepdims=True)
    capacity_ct = capacity_ct + carry * gate3
    params_ct = jnp.concatenate(
        [
            drain_ct * (0.3 * gate0 * (1.0 - gate0)),
            capacity_ct * (4.0 * gate1 * (1.0 - gate1)),
            evap_ct * (0.3 * gate2 * (1.0 - gate2)),
            carry * capacity * (gate3 * (1.0 - gate3)),
            jnp.zeros((w_out.shape[0] - 4, cells), F32),
        ],
        axis=0,
    ).astype(BF16)

    grad_out = dot(params_ct, hidden[-1], NT)
    back = dot(w_out, params_ct, TN)
    grads = [None] * layers
    for layer in range(layers - 1, -1, -1):
        top = wide[layer + 1]
        g = (back * (1.0 - top * top)).astype(BF16)
        grads[layer] = dot(hidden[layer], g, NT)
        back = dot(w_hid_ref[layer], g)
    g = (back * (1.0 - wide[0] * wide[0])).astype(BF16)
    grad_in = dot(attr, g, NT)

    rows, width = keep_ref.shape
    fill = rows - grads[1].shape[0] - grad_out.shape[0]
    first = jnp.concatenate([grads[0], grad_in], axis=0)
    second = jnp.concatenate([grads[1], grad_out, jnp.zeros((fill, width), F32)], axis=0)
    lower = lax.axis_index("cells") & 1 == 0

    @pl.when(lower)
    def _():
        keep_ref[...] = first.astype(BF16)
        send_ref[...] = second.astype(BF16)

    @pl.when(jnp.logical_not(lower))
    def _():
        keep_ref[...] = second.astype(BF16)
        send_ref[...] = first.astype(BF16)


def finish_kernel(scale, mine_ref, other_ref, grad_in_ref, grad_hid_ref, grad_out_ref):
    hid = grad_hid_ref.shape[1]
    params = grad_out_ref.shape[0]

    def place(first, second):
        grad_hid_ref[0] = first[:hid].astype(F32) * scale
        grad_in_ref[...] = first[hid:].astype(F32) * scale
        grad_hid_ref[1] = second[:hid].astype(F32) * scale
        grad_out_ref[...] = second[hid : hid + params].astype(F32) * scale

    lower = lax.axis_index("cells") & 1 == 0

    @pl.when(lower)
    def _():
        place(mine_ref, other_ref)

    @pl.when(jnp.logical_not(lower))
    def _():
        place(other_ref, mine_ref)


def exchange(block, region_flip, cells_flip):
    regions, cells = lax.axis_size("region"), lax.axis_size("cells")
    route = [
        (r * cells + c, (r ^ region_flip) * cells + (c ^ cells_flip))
        for r in range(regions)
        for c in range(cells)
    ]
    return lax.ppermute(block, ("region", "cells"), route)


def per_device(
    attributes,
    precip,
    pet_demand,
    inflow_reach,
    w_in,
    w_hid,
    w_out,
    block_inverse,
    upstream_coupling,
    discharge_cotangent,
):
    hours, cells = precip.shape
    regions, owners = lax.axis_size("region"), lax.axis_size("cells")
    attrs, hid = w_in.shape
    params = w_out.shape[1]
    reach_count = block_inverse.shape[1]
    lateral_scale = reach_count / cells
    assert 4 * cells == LANES * owners and w_hid.shape[0] == 2
    assert regions & (regions - 1) == 0 and owners & (owners - 1) == 0
    shape = jax.ShapeDtypeStruct

    def in_hbm(array):
        return pltpu.with_memory_space_constraint(array, pltpu.HBM)

    packed, ct, inverse, coupling, inflow, w_in_v, w_hid_v, w_out_v = pl.pallas_call(
        open_kernel,
        out_shape=(
            pltpu.VMEM((owners, hours, LANES), BF16),
            shape((hours, reach_count), F32),
            shape(block_inverse.shape, F32),
            shape(upstream_coupling.shape, F32),
            shape((1, cells), jnp.int32),
            shape(w_in.shape, BF16),
            shape(w_hid.shape, BF16),
            shape((16, hid), BF16),
        ),
        in_specs=[VMEM] * 10,
        out_specs=(VMEM,) * 8,
        compiler_params=pltpu.CompilerParams(vmem_limit_bytes=8 << 20),
        name="open",
    )(
        in_hbm(attributes),
        in_hbm(precip),
        in_hbm(pet_demand),
        in_hbm(discharge_cotangent),
        in_hbm(block_inverse),
        in_hbm(upstream_coupling),
        in_hbm(inflow_reach.reshape(1, cells)),
        in_hbm(w_in),
        in_hbm(w_hid),
        in_hbm(w_out.T),
    )
    arrived = lax.all_to_all(
        packed,
        "cells",
        split_axis=0,
        concat_axis=0,
        tiled=True,
        axis_index_groups=[[place(k, owners) for k in range(owners)]],
    )

    start_ct = dot_high(ct, inverse, NT)
    outgoing = dot_high(start_ct, coupling, NT)
    incoming = jnp.zeros_like(start_ct)
    for step in range(regions - 1):
        if step:
            lateral_ct = start_ct + dot_high(incoming, inverse, NT)
            outgoing = dot_high(lateral_ct, coupling, NT)
        if regions == 2:
            incoming = exchange(outgoing, 1, 0)
        else:
            incoming = shifted(outgoing, "region", -1)

    rows = hid + attrs
    runoff, keep, send = pl.pallas_call(
        functools.partial(main_kernel, lateral_scale),
        out_shape=(
            shape((hours, cells), BF16),
            shape((rows, hid), BF16),
            shape((rows, hid), BF16),
        ),
        in_specs=[VMEM] * 8,
        out_specs=(VMEM, VMEM, VMEM),
        scratch_shapes=[
            pltpu.VMEM((hours, cells), F32),
            pltpu.VMEM((hours, cells), F32),
            pltpu.VMEM((attrs, cells), F32),
            pltpu.VMEM((hours, cells), F32),
            pltpu.VMEM((hours, cells), F32),
        ],
        compiler_params=pltpu.CompilerParams(vmem_limit_bytes=32 << 20),
        name="model",
    )(arrived, start_ct, incoming, inverse, inflow, w_in_v, w_hid_v, w_out_v)

    total = keep.astype(F32) + exchange(send, 0, 1).astype(F32)
    onehot = (inflow[0][:, None] == jnp.arange(reach_count, dtype=jnp.int32)[None, :]).astype(
        BF16
    )
    lateral = dot(runoff, onehot) * lateral_scale
    discharge = dot_high(lateral, inverse)
    bits = [(1 << b, 0) for b in range(regions.bit_length() - 1)]
    bits += [(0, 1 << b) for b in range(1, owners.bit_length() - 1)]
    stages = [bits[k : k + 2] for k in range(0, len(bits), 2)]
    if regions != 2:
        for _ in range(regions - 1):
            incoming = shifted(discharge, "region", 1)
            discharge = dot_high(lateral + dot_high(incoming, coupling), inverse)
    for stage, pair in enumerate(stages):
        block = lax.optimization_barrier(total.astype(BF16))
        bundle = block
        if stage == 0 and regions == 2:
            upper = lax.reduce_precision(discharge, 8, 7)
            bundle = jnp.concatenate(
                [block, upper.astype(BF16), (discharge - upper).astype(BF16)], axis=0
            )
        first = exchange(bundle, *pair[0])
        parts = [block, first[:rows]]
        if len(pair) == 2:
            (r0, c0), (r1, c1) = pair
            parts += [exchange(block, r1, c1), exchange(block, r0 ^ r1, c0 ^ c1)]
        parts = [p.astype(F32) for p in parts]
        total = parts[0] + parts[1]
        if len(pair) == 2:
            total = total + (parts[2] + parts[3])
        if stage == 0 and regions == 2:
            upper, lower = first[rows : rows + hours], first[rows + hours :]
            incoming = upper.astype(F32) + lower.astype(F32)
            incoming = jnp.where(lax.axis_index("region") == 0, 0.0, incoming)
            discharge = dot_high(lateral + dot_high(incoming, coupling), inverse)
    total = lax.optimization_barrier(total.astype(BF16))
    other = exchange(total, 0, 1)

    grad_in, grad_hid, grad_out = pl.pallas_call(
        functools.partial(finish_kernel, 1.0 / (regions * owners)),
        out_shape=(
            shape((attrs, hid), F32),
            shape((2, hid, hid), F32),
            shape((params, hid), F32),
        ),
        in_specs=[VMEM, VMEM],
        out_specs=(VMEM, VMEM, VMEM),
        compiler_params=pltpu.CompilerParams(vmem_limit_bytes=4 << 20),
        name="finish",
    )(total, other)
    return discharge, grad_in, grad_hid, grad_out.T


def solution(mesh):
    split = ("region", "cells")
    placed = (
        P(None, split),
        P(None, split),
        P(None, split),
        P(split),
        P(),
        P(),
        P(),
        P(split, None),
        P(split, None),
        P(None, split),
    )
    return jax.shard_map(
        per_device,
        mesh=mesh,
        in_specs=placed,
        out_specs=(P(None, split), P(), P(), P()),
        check_vma=False,
    )
```
